128 devices in a mesh: dp: 32 (over y, z, core), bn: 4 (over x).
Axes of the slice: x: 4, y: 4, z: 4, core: 2. Of those that a mesh axis runs over, the one named last changes fastest.
Arguments:
- key_feats: bfloat16 [1024, 12, 16, 2048], P(('dp', 'bn')), may hold values from -22 to 22
- clip_starts: int32 [1024], P(('dp', 'bn')), may hold values from 0 to 4
- shuffle: int32 [4, 32], P('bn'), may hold values from 0 to 31, each once within a row
- query_feats: bfloat16 [1024, 2048], P(('dp', 'bn')), may hold values from -6 to 6
- conv_time: bfloat16 [3, 2048, 512], replicated, may hold values from -0.078125 to 0.078125
- conv_space: bfloat16 [9, 512, 512], replicated, may hold values from -0.09375 to 0.09375
- conv_expand: bfloat16 [512, 2048], replicated, may hold values from -0.25 to 0.25
- gain_one: float32 [512], replicated, may hold values from 0.25 to 1.75
- shift_one: float32 [512], replicated, may hold values from -3 to 3
- gain_two: float32 [512], replicated, may hold values from 0.25 to 1.75
- shift_two: float32 [512], replicated, may hold values from -3 to 3
- gain_three: float32 [2048], replicated, may hold values from 0.25 to 1.75
- shift_three: float32 [2048], replicated, may hold values from -3 to 3
- w_key: bfloat16 [2048, 128], replicated, may hold values from -0.125 to 0.125
- w_query: bfloat16 [2048, 128], replicated, may hold values from -0.125 to 0.125
- queue: bfloat16 [16384, 128], replicated, may hold values from -6 to 6
Outputs:
- keys: bfloat16 [1024, 128], P(('dp', 'bn'))
- query_grad: float32 [2048, 128], replicated
The draws below stay inside these ranges and needn't reach their ends.
Inputs may be any that keep to these rules, and one draw needn't show every extreme that they name: `shuffle`: each row is a permutation of 0 to 31.
All inputs are finite; a program needn't handle non-finite values.
Results may differ from the reference program's by a relative error of at most 0.0061.
Values may be sent and summed in bfloat16 or wider, within the bound.
A program may use at most 128 MiB of HBM per device.

```python
import jax
import jax.numpy as jnp
from jax import lax

C = 2048
INNER = 512
EMB = 128
QUEUE = 16384
FRAMES = 8
SIDE = 4
TF = 12
CLIP_DEV = 8
SPOTS = 16
PEERS = 32
GROUPS = 4
CLIPS = 1024


def draw_key_feats(key, part):
    base_key = jax.random.fold_in(key, 11)
    random_key, scale_key = jax.random.split(base_key, 2)
    extent = (CLIPS, TF, SPOTS, C)
    random_part = jnp.clip(jax.random.normal(random_key, extent, jnp.float32), -6.0, 6.0)
    clip_scale = jnp.exp(jax.random.uniform(scale_key, (CLIPS,), jnp.float32, jnp.log(0.5), jnp.log(2.0)))
    member = jnp.arange(CLIPS) // CLIP_DEV % GROUPS
    ramp_factor = 1.0 + 0.8 * member.astype(jnp.float32) / max(GROUPS - 1, 1)
    return (random_part * (clip_scale * ramp_factor)[:, None, None, None]).astype(jnp.bfloat16)


def set_ends(array, key, least, high):
    place = [jax.random.randint(jax.random.fold_in(key, axis), (), 0, length) for axis, length in enumerate(array.shape)]
    widest = array.shape.index(max(array.shape))
    next_to = place[:widest] + [(place[widest] + 1) % array.shape[widest]] + place[widest + 1:]
    return array.at[tuple(place)].set(least).at[tuple(next_to)].set(high)


def block_scale(stream_key, shape, pieces, smallest, largest):
    factor_of, own = 1.0, jax.random.fold_in(stream_key, 6)
    for position, shards_of in pieces:
        heights = jnp.exp(jax.random.uniform(jax.random.fold_in(own, position), (shards_of,), jnp.float32, smallest / len(pieces), largest / len(pieces)))
        factor_of = factor_of * jnp.repeat(heights, shape[position] // shards_of).reshape([-1 if axis == position else 1 for axis in range(len(shape))])
    return factor_of


def normal_values(rng, dims, width, limit, cuts=(), kind=jnp.bfloat16):
    entries = width * jax.random.normal(rng, dims, jnp.float32)
    if cuts:
        entries = entries * block_scale(rng, dims, cuts, -0.22, 0.18)
    return jnp.clip(entries, -limit, limit).astype(kind)


def setup_inputs(seed: int = 0) -> dict:
    key_list = jax.random.split(jax.random.key(seed), 17)
    key_feats = draw_key_feats(jax.random.fold_in(key_list[16], 71), 0)
    clip_starts = set_ends(jax.random.randint(key_list[1], (CLIPS,), 0, TF - FRAMES + 1), jax.random.fold_in(key_list[1], 1), 0, TF - FRAMES).astype(jnp.int32)
    shuffle = jax.vmap(lambda own: jax.random.permutation(own, PEERS))(jax.random.split(key_list[2], GROUPS)).reshape((GROUPS, PEERS)).astype(jnp.int32)
    query_feats = normal_values(key_list[3], (CLIPS, C), 1.0, 6.0, ((0, 128),))
    conv_time = normal_values(key_list[4], (3, C, INNER), (3 * C) ** -0.5, 0.078125)
    conv_space = normal_values(key_list[5], (9, INNER, INNER), (9 * INNER) ** -0.5, 0.09375)
    conv_expand = normal_values(key_list[6], (INNER, C), INNER ** -0.5, 0.25)
    gain_one = jnp.clip(1.0 + 0.15 * jax.random.normal(key_list[7], (INNER,), jnp.float32), 0.25, 1.75)
    shift_one = normal_values(key_list[8], (INNER,), 0.5, 3.0, (), jnp.float32)
    gain_two = jnp.clip(1.0 + 0.15 * jax.random.normal(key_list[9], (INNER,), jnp.float32), 0.25, 1.75)
    shift_two = normal_values(key_list[10], (INNER,), 0.5, 3.0, (), jnp.float32)
    gain_three = jnp.clip(1.0 + 0.15 * jax.random.normal(key_list[11], (C,), jnp.float32), 0.25, 1.75)
    shift_three = normal_values(key_list[12], (C,), 0.5, 3.0, (), jnp.float32)
    w_key = normal_values(key_list[13], (C, EMB), C ** -0.5, 0.125)
    w_query = normal_values(key_list[14], (C, EMB), C ** -0.5, 0.125)
    queue = normal_values(key_list[15], (QUEUE, EMB), 1.0, 6.0)
    return dict(key_feats=key_feats, clip_starts=clip_starts, shuffle=shuffle, query_feats=query_feats, conv_time=conv_time, conv_space=conv_space, conv_expand=conv_expand, gain_one=gain_one, shift_one=shift_one, gain_two=gain_two, shift_two=shift_two, gain_three=gain_three, shift_three=shift_three, w_key=w_key, w_query=w_query, queue=queue)


SHARPNESS_DIVISOR = 0.2
EPSILON = 1e-05

def pick_frames(features, starts):

    def single(clip_feats, first_frame):
        return lax.dynamic_slice_in_dim(clip_feats, first_frame, FRAMES, 0)
    return jax.vmap(single)(features, starts.astype(jnp.int32))

def time_conv(values, weights):
    padded = jnp.pad(values.astype(jnp.float32), ((0, 0), (1, 1), (0, 0), (0, 0)))
    length = values.shape[1]
    summed = jnp.zeros(values.shape[:3] + (weights.shape[2],), jnp.float32)
    for offset in range(3):
        summed = summed + jnp.einsum('afsc,cd->afsd', padded[:, offset:offset + length], weights[offset].astype(jnp.float32))
    return summed

def space_conv(values, weights):
    square_grid = values.astype(jnp.float32).reshape(values.shape[0], values.shape[1], SIDE, SIDE, values.shape[3])
    padded = jnp.pad(square_grid, ((0, 0), (0, 0), (1, 1), (1, 1), (0, 0)))
    summed = jnp.zeros((values.shape[0], values.shape[1], SIDE, SIDE, weights.shape[2]), jnp.float32)
    for row_shift in range(3):
        for col_shift in range(3):
            window = padded[:, :, row_shift:row_shift + SIDE, col_shift:col_shift + SIDE]
            summed = summed + jnp.einsum('afhwc,cd->afhwd', window, weights[3 * row_shift + col_shift].astype(jnp.float32))
    return summed.reshape(values.shape[0], values.shape[1], SIDE * SIDE, weights.shape[2])

def batch_norm(values, total_sum, squares, row_count, gain_row, shift_row):
    center = total_sum / row_count
    spread = squares / row_count - center * center
    return (values - center) * (gain_row * lax.rsqrt(spread + EPSILON)) + shift_row

def local_moments(values):
    return (lax.optimization_barrier(jnp.sum(values, axis=(0, 1, 2))), lax.optimization_barrier(jnp.sum(values * values, axis=(0, 1, 2))))

def encode(values, params, moments, row_count):
    conv_time, conv_space, conv_expand, gain_one, shift_one, gain_two, shift_two, gain_three, shift_three, w_key = params
    first_out = time_conv(values, conv_time)
    total_sum, squares = moments(first_out)
    act_one = jnp.maximum(batch_norm(first_out, total_sum, squares, row_count, gain_one, shift_one), 0.0).astype(jnp.bfloat16)
    second = space_conv(act_one, conv_space)
    total_sum, squares = moments(second)
    act_two = jnp.maximum(batch_norm(second, total_sum, squares, row_count, gain_two, shift_two), 0.0).astype(jnp.bfloat16)
    third_out = jnp.einsum('afsc,cd->afsd', act_two.astype(jnp.float32), conv_expand.astype(jnp.float32))
    total_sum, squares = moments(third_out)
    merged = jnp.maximum(batch_norm(third_out, total_sum, squares, row_count, gain_three, shift_three) + values.astype(jnp.float32), 0.0)
    pooled = lax.optimization_barrier(jnp.mean(merged, axis=(1, 2))).astype(jnp.bfloat16)
    projected = jnp.dot(pooled, w_key, preferred_element_type=jnp.float32)
    return (projected * lax.rsqrt(lax.optimization_barrier(jnp.sum(projected * projected, axis=-1, keepdims=True)) + 1e-06)).astype(jnp.bfloat16)

def query_terms(query_feats, own_keys, w_query, queue):
    projected = jnp.dot(query_feats, w_query, preferred_element_type=jnp.float32)
    length = jnp.sqrt(lax.optimization_barrier(jnp.sum(projected * projected, axis=-1, keepdims=True)) + 1e-06)
    anchor_direction = projected / length
    queue_wide = queue.astype(jnp.float32)
    memory_bank_directions = (queue_wide * lax.rsqrt(lax.optimization_barrier(jnp.sum(queue_wide * queue_wide, axis=-1, keepdims=True)) + 1e-06)).astype(jnp.bfloat16)
    collected_encodings = own_keys.astype(jnp.float32)
    matching_scores = lax.optimization_barrier(jnp.sum(anchor_direction * collected_encodings, axis=-1)) / SHARPNESS_DIVISOR
    distractor_scores = jnp.einsum('nf,ef->ne', anchor_direction.astype(jnp.bfloat16).astype(jnp.float32), memory_bank_directions.astype(jnp.float32)) / SHARPNESS_DIVISOR
    partition = jnp.exp(matching_scores) + lax.optimization_barrier(jnp.sum(jnp.exp(distractor_scores), axis=-1))
    log_total = jnp.log(partition)
    weight_pos = jnp.exp(matching_scores - log_total)
    weight_neg = jnp.exp(distractor_scores - log_total[:, None]).astype(jnp.bfloat16)
    retrieved_samples = jnp.dot(weight_neg, memory_bank_directions, preferred_element_type=jnp.float32) + (weight_pos - 1.0)[:, None] * collected_encodings
    anchor_loss_derivative = retrieved_samples / SHARPNESS_DIVISOR
    radial = lax.optimization_barrier(jnp.sum(anchor_direction * anchor_loss_derivative, axis=-1, keepdims=True))
    grad_proj = ((anchor_loss_derivative - radial * anchor_direction) / length).astype(jnp.bfloat16)
    return jnp.einsum('nc,ne->ce', query_feats.astype(jnp.float32), grad_proj.astype(jnp.float32))

def reference(key_feats, clip_starts, shuffle, query_feats, conv_time, conv_space, conv_expand, gain_one, shift_one, gain_two, shift_two, gain_three, shift_three, w_key, w_query, queue):
    params = (conv_time, conv_space, conv_expand, gain_one, shift_one, gain_two, shift_two, gain_three, shift_three, w_key)
    positions = jnp.arange(PEERS, dtype=jnp.int32)
    matches = (shuffle[:, :, None] == positions[None, None, :]).astype(jnp.int32)
    inverse = lax.optimization_barrier(jnp.sum(positions[None, :, None] * matches, axis=1)).astype(jnp.int32)

    def group_keys(host_group):
        members = []
        for member in range(GROUPS):
            source = inverse[member, host_group]
            first_clip = ((source * GROUPS + member) * CLIP_DEV).astype(jnp.int32)
            clip_feats = lax.dynamic_slice_in_dim(key_feats, first_clip, CLIP_DEV, 0)
            starts = lax.dynamic_slice_in_dim(clip_starts, first_clip, CLIP_DEV, 0)
            members.append(pick_frames(clip_feats, starts))
        values = jnp.concatenate(members, axis=0)
        row_count = values.shape[0] * values.shape[1] * values.shape[2]
        encoded = encode(values, params, local_moments, row_count)
        return encoded.reshape(GROUPS, CLIP_DEV, EMB)
    hosted = lax.map(group_keys, positions)
    returned = jnp.stack([jnp.take(hosted[:, member], shuffle[member], axis=0) for member in range(GROUPS)], axis=1)
    own_keys = returned.reshape(CLIPS, EMB)
    query_grad = query_terms(query_feats, own_keys, w_query, queue)
    return (own_keys, query_grad)
```

```python
import jax
import jax.numpy as jnp
from jax import lax
from jax.sharding import PartitionSpec as P

FRAMES = 8
SIDE = 4


SHARPNESS_DIVISOR = 0.2
EPSILON = 1e-05


def pick_frames(features, starts):

    def single(clip_feats, first_frame):
        return lax.dynamic_slice_in_dim(clip_feats, first_frame, FRAMES, 0)

    return jax.vmap(single)(features, starts)


def time_conv(values, weights):
    padded = jnp.pad(values, ((0, 0), (1, 1), (0, 0), (0, 0)))
    length = values.shape[1]
    summed = jnp.zeros(values.shape[:3] + (weights.shape[2],), jnp.float32)
    for offset in range(3):
        summed = summed + jnp.einsum(
            "afsc,cd->afsd",
            padded[:, offset : offset + length],
            weights[offset],
            preferred_element_type=jnp.float32,
        )
    return summed


def space_conv(values, weights):
    square_grid = values.reshape(values.shape[0], values.shape[1], SIDE, SIDE, values.shape[3])
    padded = jnp.pad(square_grid, ((0, 0), (0, 0), (1, 1), (1, 1), (0, 0)))
    summed = jnp.zeros(
        (values.shape[0], values.shape[1], SIDE, SIDE, weights.shape[2]), jnp.float32
    )
    for row_shift in range(3):
        for col_shift in range(3):
            window = padded[:, :, row_shift : row_shift + SIDE, col_shift : col_shift + SIDE]
            summed = summed + jnp.einsum(
                "afhwc,cd->afhwd",
                window,
                weights[3 * row_shift + col_shift],
                preferred_element_type=jnp.float32,
            )
    return summed.reshape(values.shape[0], values.shape[1], SIDE * SIDE, weights.shape[2])


def batch_norm(values, total_sum, squares, row_count, gain_row, shift_row):
    center = total_sum / row_count
    spread = squares / row_count - center * center
    return (values - center) * (gain_row * lax.rsqrt(spread + EPSILON)) + shift_row


def encode(values, params, moments, row_count):
    (
        conv_time,
        conv_space,
        conv_expand,
        gain_one,
        shift_one,
        gain_two,
        shift_two,
        gain_three,
        shift_three,
        w_key,
    ) = params
    first_out = time_conv(values, conv_time)
    total_sum, squares = moments(first_out)
    act_one = jnp.maximum(
        batch_norm(first_out, total_sum, squares, row_count, gain_one, shift_one), 0.0
    ).astype(jnp.bfloat16)
    second = space_conv(act_one, conv_space)
    total_sum, squares = moments(second)
    act_two = jnp.maximum(
        batch_norm(second, total_sum, squares, row_count, gain_two, shift_two), 0.0
    ).astype(jnp.bfloat16)
    third_out = jnp.einsum(
        "afsc,cd->afsd", act_two, conv_expand, preferred_element_type=jnp.float32
    )
    total_sum, squares = moments(third_out)
    merged = jnp.maximum(
        batch_norm(third_out, total_sum, squares, row_count, gain_three, shift_three)
        + values.astype(jnp.float32),
        0.0,
    )
    pooled = jnp.mean(merged, axis=(1, 2)).astype(jnp.bfloat16)
    projected = jnp.dot(pooled, w_key, preferred_element_type=jnp.float32)
    return (
        projected * lax.rsqrt(jnp.sum(projected * projected, axis=-1, keepdims=True) + 1e-06)
    ).astype(jnp.bfloat16)


def query_terms(query_feats, own_keys, w_query, queue):
    projected = jnp.dot(query_feats, w_query, preferred_element_type=jnp.float32)
    length = jnp.sqrt(jnp.sum(projected * projected, axis=-1, keepdims=True) + 1e-06)
    anchor_direction = projected / length
    queue_wide = queue.astype(jnp.float32)
    memory_bank_directions = (
        queue_wide * lax.rsqrt(jnp.sum(queue_wide * queue_wide, axis=-1, keepdims=True) + 1e-06)
    ).astype(jnp.bfloat16)
    collected_encodings = own_keys.astype(jnp.float32)
    matching_scores = jnp.sum(anchor_direction * collected_encodings, axis=-1) / SHARPNESS_DIVISOR
    distractor_scores = (
        jnp.einsum(
            "nf,ef->ne",
            anchor_direction.astype(jnp.bfloat16),
            memory_bank_directions,
            preferred_element_type=jnp.float32,
        )
        / SHARPNESS_DIVISOR
    )
    partition = jnp.exp(matching_scores) + jnp.sum(jnp.exp(distractor_scores), axis=-1)
    log_total = jnp.log(partition)
    weight_pos = jnp.exp(matching_scores - log_total)
    weight_neg = jnp.exp(distractor_scores - log_total[:, None]).astype(jnp.bfloat16)
    retrieved_samples = (
        jnp.dot(weight_neg, memory_bank_directions, preferred_element_type=jnp.float32)
        + (weight_pos - 1.0)[:, None] * collected_encodings
    )
    anchor_loss_derivative = retrieved_samples / SHARPNESS_DIVISOR
    radial = jnp.sum(anchor_direction * anchor_loss_derivative, axis=-1, keepdims=True)
    return ((anchor_loss_derivative - radial * anchor_direction) / length).astype(jnp.bfloat16)


def local(
    key_feats,
    clip_starts,
    shuffle,
    query_feats,
    conv_time,
    conv_space,
    conv_expand,
    gain_one,
    shift_one,
    gain_two,
    shift_two,
    gain_three,
    shift_three,
    w_key,
    w_query,
    queue,
):
    params = (
        conv_time,
        conv_space,
        conv_expand,
        gain_one,
        shift_one,
        gain_two,
        shift_two,
        gain_three,
        shift_three,
        w_key,
    )
    chosen = pick_frames(key_feats, clip_starts)
    peer_count = lax.axis_size("dp")
    groups = lax.axis_size("bn")
    target = shuffle[0, lax.axis_index("dp")]
    row_count = groups * chosen.shape[0] * chosen.shape[1] * chosen.shape[2]
    slot = (jnp.arange(peer_count, dtype=jnp.int32) == target).astype(jnp.float32)

    def group_moments(values):
        sums = jnp.stack([jnp.sum(values, axis=(0, 1, 2)), jnp.sum(values * values, axis=(0, 1, 2))])
        table = lax.psum(slot[:, None, None] * sums[None], ("dp", "bn"))
        own = lax.dynamic_index_in_dim(table, target, 0, keepdims=False)
        return own[0], own[1]

    own_keys = encode(chosen, params, group_moments, row_count)
    grad_proj = query_terms(query_feats, own_keys, w_query, queue)
    grad_part = jnp.einsum("nc,ne->ce", query_feats, grad_proj, preferred_element_type=jnp.float32)
    query_grad = lax.psum(grad_part, ("dp", "bn"))
    return (own_keys, query_grad)


def solution(mesh):
    placed = (
        P(("dp", "bn"), None, None, None),
        P(("dp", "bn")),
        P("bn", None),
        P(("dp", "bn"), None),
        P(),
        P(),
        P(),
        P(),
        P(),
        P(),
        P(),
        P(),
        P(),
        P(),
        P(),
        P(),
    )
    return jax.shard_map(
        local, mesh=mesh, in_specs=placed, out_specs=(P(("dp", "bn"), None), P()), check_vma=False
    )
```

```python
import jax
import jax.numpy as jnp
from jax import lax
from jax.experimental import pallas as pl
from jax.experimental.pallas import tpu as pltpu
from jax.sharding import PartitionSpec as P

MESH = pl.DeviceIdType.MESH
F32, BF16, I32 = jnp.float32, jnp.bfloat16, jnp.int32
CLIPS, FRAMES, TF, SPOTS, SIDE = 8, 8, 12, 16, 4
C, INNER, EMB, QUEUE = 2048, 512, 128, 16384
PLANE, LINE, PEERS = 16, 8, 32
KC = 512
NK = C // KC
ROWS = CLIPS * FRAMES * SPOTS
COUNT = float(4 * ROWS)
EPS, TINY = 1e-05, 1e-06
PARTS = ((0, 640), (640, 640), (1280, 768))
ORDER = ((2, 1, 0), (1, 0, 2), (0, 2, 1))


def await_bytes(ref, sem):
    pltpu.make_async_copy(ref, ref, sem).wait()


def kernel(
    starts, feats, shuf, qf_h, wt_h, ws_h, we_h, g1, s1, g2, s2, g3, s3, wk_h, wq_h, queue_h,
    keys_out, grad_out,
    xall, xc, wt, acc, act, ws, act2, we, third, queue_v, qall, qt, wk, wq,
    tabv, tabs, picks, sb1, sb3, ra1, ra3, tb1, tb3, rb1, rb3, qmine, gall, pooled, gvec,
    hsem, asem, bsem, gsem, tsem, qsem, csem,
):
    i, x = lax.axis_index("dp"), lax.axis_index("bn")
    yz, core = i // 2, i % 2
    y, z = yz // 4, yz % 4
    xyz = (x, y, z)
    member = x * 2 + core
    half = core * 4 + x
    gall_plane = gall.at[0, pl.ds(0, PLANE - 1)]
    gall_line = gall.at[pl.ds(0, LINE - 1)]

    def plane_peer(k):
        return ((yz + k) % PLANE * 2 + core, x)

    def line_peer(k):
        m = (member + k) % LINE
        return (yz * 2 + m % 2, m // 2)

    def axis_peer(axis, k):
        c = list(xyz)
        c[axis] = (c[axis] + k) % 4
        return ((c[1] * 4 + c[2]) * 2 + core, c[0])

    barrier = pltpu.get_barrier_semaphore()
    for k in range(1, PLANE):
        pl.semaphore_signal(barrier, inc=1, device_id=plane_peer(k), device_id_type=MESH)
    for k in range(1, LINE):
        pl.semaphore_signal(barrier, inc=1, device_id=line_peer(k), device_id_type=MESH)

    def load(src, dst, n):
        return pltpu.make_async_copy(src, dst, hsem.at[n])

    own_q = qall.at[core, x, y, z]
    feat_loads = [load(feats.at[:, :, :, pl.ds(KC * k, KC)], xall[k], k) for k in range(NK)]
    wt_loads = [load(wt_h.at[:, pl.ds(KC * k, KC), :], wt.at[k], NK + k) for k in range(NK)]
    small = [load(qf_h, own_q, 8), load(qf_h, qmine, 9), load(wq_h, wq, 10)]
    queue_load = load(queue_h, queue_v, 11)
    ws_load = load(ws_h, ws, 12)
    we_load = load(we_h, we, 13)
    wk_load = load(wk_h, wk, 14)
    for k in range(2):
        feat_loads[k].start()
        wt_loads[k].start()
    for d in small:
        d.start()

    row = shuf[...].astype(F32)
    sq = (PEERS, PEERS)
    r_i = lax.broadcasted_iota(I32, sq, 0)
    c_i = lax.broadcasted_iota(I32, sq, 1)
    wide = jnp.broadcast_to(row, sq)
    column = jnp.sum(jnp.where(r_i == c_i, wide, 0.0), axis=1, keepdims=True)
    hit = column == c_i.astype(F32)
    inverse = jnp.sum(jnp.where(hit, r_i.astype(F32), 0.0), axis=0, keepdims=True)
    tabv[x] = jnp.zeros((8, 128), I32)
    tabv[4] = jnp.zeros((8, 128), I32)
    tabv[x, 0:1, 0:PEERS] = shuf[...]
    tabv[4, 0:1, 0:PEERS] = inverse.astype(I32)

    for k in range(NK):
        for e in (0, FRAMES + 1):
            xc[k, :, e] = jnp.zeros((CLIPS, SPOTS, KC), BF16)

    def conv_one(k):
        def pick(n, _):
            first = starts[n]
            for t in range(FRAMES):
                xc[k, n, 1 + t] = xall[k][n, first + t]
            return 0

        lax.fori_loop(0, CLIPS, pick, 0)

        def rows(p, _):
            lhs = jnp.concatenate(
                [xc[k, pl.ds(2 * p, 2), o : o + FRAMES].reshape(256, KC) for o in range(3)], axis=1
            )
            r = jnp.dot(lhs, wt[k].reshape(3 * KC, INNER), preferred_element_type=F32)
            at = pl.ds(pl.multiple_of(p * 256, 256), 256)
            for q in range(4):
                v = r[:, 128 * q : 128 * (q + 1)]
                acc[q, at, :] = v if k == 0 else acc[q, at, :] + v
            return 0

        lax.fori_loop(0, CLIPS // 2, rows, 0)

    def q_region(p, done):
        at = [pl.ds(xyz[a], 1) for a in range(3)]
        for a in done:
            at[a] = pl.ds(0, 4)
        return qall.at[(core, *at, slice(None), pl.ds(*PARTS[p]))]

    def q_send(phase):
        for p in range(3):
            part = q_region(p, ORDER[p][:phase])
            for k in range(1, 4):
                pltpu.make_async_remote_copy(
                    src_ref=part, dst_ref=part, send_sem=qsem.at[0, p, phase], recv_sem=qsem.at[1, p, phase],
                    device_id=axis_peer(ORDER[p][phase], k), device_id_type=MESH,
                ).start()

    def q_wait(phase, side):
        for p in range(3):
            cols = pl.ds(*PARTS[p])
            ref = (
                qall.at[0, 0, 0, pl.ds(0, 3), :, cols],
                qall.at[0, 0, pl.ds(0, 3), :, :, cols],
                qall.at[0, pl.ds(0, 3), :, :, :, cols],
            )[phase]
            await_bytes(ref, qsem.at[side, p, phase])

    core_copy = pltpu.make_async_remote_copy(
        src_ref=qall.at[core], dst_ref=qall.at[core], send_sem=csem.at[0], recv_sem=csem.at[1],
        device_id=(yz * 2 + 1 - core, x), device_id_type=MESH,
    )

    def plane_send(r, sb, ra):
        for k in range(1, PLANE):
            pltpu.make_async_remote_copy(
                src_ref=sb.at[...], dst_ref=ra.at[k - 1], send_sem=asem.at[0, r], recv_sem=asem.at[1, r],
                device_id=plane_peer(k), device_id_type=MESH,
            ).start()

    def plane_finish(r, sb, ra, tb, rb):
        ra[PLANE - 1] = sb[...]
        await_bytes(ra.at[pl.ds(0, PLANE - 1)], asem.at[1, r])
        mine = None
        for k in range(LINE):
            v = ra[picks[0, k]] * jnp.where(picks[1, k] == 1, 1.0, 0.0).astype(F32)
            if k == 0:
                mine = v
                continue
            tb[k - 1] = v
            pltpu.make_async_remote_copy(
                src_ref=tb.at[k - 1], dst_ref=rb.at[k - 1], send_sem=bsem.at[0, r], recv_sem=bsem.at[1, r],
                device_id=line_peer(k), device_id_type=MESH,
            ).start()
        await_bytes(rb.at[pl.ds(0, LINE - 1)], bsem.at[1, r])
        for k in range(LINE - 1):
            mine = mine + rb[k]
        return mine

    def put_stats(dst, total, squares):
        for q in range(4):
            dst[q : q + 1, :] = total[:, 128 * q : 128 * (q + 1)]
            dst[4 + q : 5 + q, :] = squares[:, 128 * q : 128 * (q + 1)]

    def affine(tile, gain, shift):
        scales, shifts = [], []
        for q in range(4):
            m = tile[q : q + 1, :] * (1.0 / COUNT)
            w = tile[4 + q : 5 + q, :] * (1.0 / COUNT) - m * m
            scale = gain[:, 128 * q : 128 * (q + 1)] * lax.rsqrt(w + EPS)
            scales.append(scale)
            shifts.append(shift[:, 128 * q : 128 * (q + 1)] - m * scale)
        return jnp.concatenate(scales, axis=1), jnp.concatenate(shifts, axis=1)

    def sums_of(block):
        v = block.reshape(-1, 8, INNER)
        return jnp.sum(v, axis=0), jnp.sum(v * v, axis=0)

    def rows_of(ref, at):
        return jnp.concatenate([ref[q, at, :] for q in range(4)], axis=1)

    def total_of(ref):
        def body(p, carry):
            a, b = sums_of(rows_of(ref, pl.ds(pl.multiple_of(p * 128, 128), 128)))
            return carry[0] + a, carry[1] + b

        zero = jnp.zeros((8, INNER), F32)
        a, b = lax.fori_loop(0, ROWS // 128, body, (zero, zero))
        return jnp.sum(a, axis=0, keepdims=True), jnp.sum(b, axis=0, keepdims=True)

    for k in range(NK):
        feat_loads[k].wait()
        wt_loads[k].wait()
        if k + 2 < NK:
            feat_loads[k + 2].start()
            wt_loads[k + 2].start()
        if k == 1:
            queue_load.start()
            ws_load.start()
        if k == 2:
            we_load.start()
            wk_load.start()
        conv_one(k)
        if k == 0:
            pl.semaphore_wait(barrier, PLANE - 1 + LINE - 1)
            for d in small:
                d.wait()
            for n in range(1, 4):
                pltpu.make_async_remote_copy(
                    src_ref=tabv.at[x], dst_ref=tabv.at[x], send_sem=tsem.at[0], recv_sem=tsem.at[1],
                    device_id=axis_peer(0, n), device_id_type=MESH,
                ).start()
            q_send(0)
        if k == 2:
            q_wait(0, 1)
            q_send(1)
    put_stats(sb1.at[0, 0], *total_of(acc))
    plane_send(0, sb1.at[0], ra1[0])

    await_bytes(tabv.at[pl.ds(0, 3)], tsem.at[1])
    to_scalar = pltpu.make_async_copy(tabv, tabs, hsem.at[15])
    to_scalar.start()
    to_scalar.wait()
    for k in range(LINE):
        m = (member + k) % LINE
        group = tabs[m // 2, 0, yz * 2 + m % 2]
        j = tabs[4, 0, group]
        picks[0, k] = (yz - j // 2 + PLANE - 1) % PLANE
        picks[1, k] = jnp.where(j % 2 == core, 1, 0).astype(I32)

    zq = jnp.dot(qmine[...], wq[...], preferred_element_type=F32)
    length = jnp.sqrt(jnp.sum(zq * zq, axis=-1, keepdims=True) + TINY)
    unit = zq / length
    unit_b = unit.astype(BF16)
    queue_load.wait()

    def queue_part(lo, hi, carry):
        def body(n, carry):
            total, mix = carry
            qb = queue_v[pl.ds(pl.multiple_of(n * 1024, 1024), 1024), :].astype(F32)
            inv = lax.rsqrt(jnp.sum(qb * qb, axis=-1, keepdims=True) + TINY)
            qu = (qb * inv).astype(BF16)
            neg = lax.dot_general(unit_b, qu, (((1,), (1,)), ((), ())), preferred_element_type=F32) * 5.0
            e = jnp.exp(neg)
            total = total + jnp.sum(e, axis=-1, keepdims=True)
            mix = mix + jnp.dot(e.astype(BF16), qu, preferred_element_type=F32)
            return total, mix

        return lax.fori_loop(lo, hi, body, carry)

    carry = (jnp.zeros((CLIPS, 1), F32), jnp.zeros((CLIPS, EMB), F32))
    carry = queue_part(0, 8, carry)

    tile = plane_finish(0, sb1.at[0], ra1[0], tb1.at[0], rb1.at[0])
    q_wait(1, 1)
    q_send(2)

    scale, shift = affine(tile[0], g1[...], s1[...])
    for r in range(4):
        for e in (0, SIDE + 1):
            act[r, e] = jnp.zeros((64, INNER), BF16)

    def norm_one(p, _):
        for r in range(SIDE):
            for c in range(SIDE):
                both = [
                    rows_of(acc, pl.ds((2 * p + h) * 128 + SIDE * r + c, FRAMES, stride=SPOTS)) for h in range(2)
                ]
                v = jnp.concatenate(both, axis=0)
                v = jnp.maximum(v * scale + shift, 0.0).astype(BF16)
                act[r, c + 1, pl.ds(pl.multiple_of(p * 16, 16), 16), :] = v
        return 0

    lax.fori_loop(0, CLIPS // 2, norm_one, 0)

    ws_load.wait()

    def row_conv(r, base, tap, taps):
        lhs = jnp.concatenate(
            [act[base + d, c : c + SIDE].reshape(256, INNER) for d in range(taps) for c in range(3)], axis=1
        )
        w = ws[pl.ds(tap, 3 * taps)].reshape(3 * taps * INNER, INNER)
        v = jnp.dot(lhs, w, preferred_element_type=F32)
        for q in range(4):
            acc[q, pl.ds(pl.multiple_of(r * 256, 256), 256), :] = v[:, 128 * q : 128 * (q + 1)]

    def edge(n, _):
        row_conv(3 * n, 2 * n, 3 - 3 * n, 2)
        return 0

    def middle(n, _):
        row_conv(1 + n, n, 0, 3)
        return 0

    lax.fori_loop(0, 2, edge, 0)
    lax.fori_loop(0, 2, middle, 0)
    put_stats(sb1.at[1, 0], *total_of(acc))
    plane_send(1, sb1.at[1], ra1[1])
    carry = queue_part(8, 16, carry)
    tile = plane_finish(1, sb1.at[1], ra1[1], tb1.at[1], rb1.at[1])

    scale, shift = affine(tile[0], g2[...], s2[...])

    def norm_two(p, _):
        for h in range(8):
            v = rows_of(acc, pl.ds(p * 8 + h, SPOTS, stride=64))
            act2[pl.ds(pl.multiple_of(p * 128, 128) + h * 16, 16), :] = jnp.maximum(
                v * scale + shift, 0.0
            ).astype(BF16)
        return 0

    lax.fori_loop(0, CLIPS, norm_two, 0)
    we_load.wait()

    def expand(q, _):
        def body(p, carry):
            at = pl.ds(pl.multiple_of(p * 256, 256), 256)
            cols = pl.ds(pl.multiple_of(q * INNER, INNER), INNER)
            r = jnp.dot(act2[at, :], we[:, cols], preferred_element_type=F32)
            third[q, at, :] = r
            a, b = sums_of(r)
            return carry[0] + a, carry[1] + b

        zero = jnp.zeros((8, INNER), F32)
        a, b = lax.fori_loop(0, 4, body, (zero, zero))
        put_stats(sb3.at[q], jnp.sum(a, axis=0, keepdims=True), jnp.sum(b, axis=0, keepdims=True))
        return 0

    lax.fori_loop(0, 4, expand, 0)
    plane_send(2, sb3, ra3)
    q_wait(2, 1)
    core_copy.start()
    tile = plane_finish(2, sb3, ra3, tb3, rb3)

    for q in range(4):
        cols = slice(INNER * q, INNER * (q + 1))
        scale, shift = affine(tile[q], g3[:, cols], s3[:, cols])

        def pool(n, _):
            v = third[q, pl.ds(pl.multiple_of(n * 128, 128), 128), :]
            kept = xc[q, n, 1 : 1 + FRAMES].reshape(128, KC).astype(F32)
            v = jnp.maximum(v * scale + shift + kept, 0.0)
            part = jnp.sum(v.reshape(16, 8, INNER), axis=0)
            pooled[pl.ds(n, 1), cols] = jnp.sum(part, axis=0, keepdims=True) * (1.0 / 128.0)
            return 0

        lax.fori_loop(0, CLIPS, pool, 0)
    wk_load.wait()
    projected = jnp.dot(pooled[...].astype(BF16), wk[...], preferred_element_type=F32)
    norm = jnp.sum(projected * projected, axis=-1, keepdims=True) + TINY
    keys = (projected * lax.rsqrt(norm)).astype(BF16)
    keys_out[...] = keys

    held = keys.astype(F32)
    total, mix = carry
    e_pos = jnp.exp(jnp.sum(unit * held, axis=-1, keepdims=True) * 5.0)
    whole = e_pos + total
    grad = (mix / whole + (e_pos / whole - 1.0) * held) * 5.0
    radial = jnp.sum(unit * grad, axis=-1, keepdims=True)
    gvec[...] = ((grad - radial * unit) / length).astype(BF16)
    for k in range(1, PLANE):
        pltpu.make_async_remote_copy(
            src_ref=gvec, dst_ref=gall.at[half, yz], send_sem=gsem.at[0], recv_sem=gsem.at[1],
            device_id=plane_peer(k), device_id_type=MESH,
        ).start()
    gall[half, yz] = gvec[...]
    core_copy.wait_recv()

    def turn(n, _):
        cols = pl.ds(pl.multiple_of(n * 128, 128), 128)
        v = qall[:, :, :, :, :, cols].astype(F32).reshape(1024, 128)
        qt[cols, :] = v.T.astype(BF16)
        return 0

    lax.fori_loop(0, C // 128, turn, 0)
    await_bytes(gall_plane, gsem.at[1])
    for k in range(1, LINE):
        pltpu.make_async_remote_copy(
            src_ref=gall.at[half], dst_ref=gall.at[half], send_sem=gsem.at[2], recv_sem=gsem.at[3],
            device_id=line_peer(k), device_id_type=MESH,
        ).start()
    await_bytes(gall_line, gsem.at[3])
    g_all = gall[...].astype(F32).reshape(1024, EMB).astype(BF16)

    def last(n, _):
        at = pl.ds(pl.multiple_of(n * 256, 256), 256)
        grad_out[at, :] = jnp.dot(qt[at, :], g_all, preferred_element_type=F32)
        return 0

    lax.fori_loop(0, C // 256, last, 0)

    await_bytes(tabv.at[pl.ds(0, 3)], tsem.at[0])
    for phase in range(3):
        q_wait(phase, 0)
    core_copy.wait_send()
    for r, ra, rb in ((0, ra1[0], rb1.at[0]), (1, ra1[1], rb1.at[1]), (2, ra3, rb3)):
        await_bytes(ra.at[pl.ds(0, PLANE - 1)], asem.at[0, r])
        await_bytes(rb.at[pl.ds(0, LINE - 1)], bsem.at[0, r])
    await_bytes(gall_plane, gsem.at[0])
    await_bytes(gall_line, gsem.at[2])


def local(
    key_feats, clip_starts, shuffle, query_feats, conv_time, conv_space, conv_expand,
    gain_one, shift_one, gain_two, shift_two, gain_three, shift_three, w_key, w_query, queue,
):
    vmem = pl.BlockSpec(memory_space=pltpu.VMEM)
    smem = pl.BlockSpec(memory_space=pltpu.SMEM)
    hbm = pl.BlockSpec(memory_space=pltpu.HBM)
    V = pltpu.VMEM
    DMA = pltpu.SemaphoreType.DMA
    rows = [v.reshape(1, -1) for v in (gain_one, shift_one, gain_two, shift_two, gain_three, shift_three)]
    return pl.pallas_call(
        kernel,
        name="moco",
        out_shape=(
            jax.ShapeDtypeStruct((CLIPS, EMB), BF16),
            jax.ShapeDtypeStruct((C, EMB), F32),
        ),
        in_specs=[smem, hbm, vmem, hbm, hbm, hbm, hbm] + [vmem] * 6 + [hbm] * 3,
        out_specs=(vmem, vmem),
        scratch_shapes=[
            [V((CLIPS, TF, SPOTS, KC), BF16) for _ in range(NK)],
            V((NK, CLIPS, FRAMES + 2, SPOTS, KC), BF16),
            V((NK, 3, KC, INNER), BF16),
            V((4, ROWS, 128), F32),
            V((SIDE, SIDE + 2, 64, INNER), BF16),
            V((9, INNER, INNER), BF16),
            V((ROWS, INNER), BF16),
            V((INNER, C), BF16),
            V((4, ROWS, INNER), F32),
            V((QUEUE, EMB), BF16),
            V((2, 4, 4, 4, CLIPS, C), BF16),
            V((C, 1024), BF16),
            V((C, EMB), BF16),
            V((C, EMB), BF16),
            V((5, 8, 128), I32),
            pltpu.SMEM((5, 8, 128), I32),
            pltpu.SMEM((2, LINE), I32),
            V((2, 1, 8, 128), F32),
            V((4, 8, 128), F32),
            [V((PLANE, 1, 8, 128), F32) for _ in range(2)],
            V((PLANE, 4, 8, 128), F32),
            V((2, LINE - 1, 1, 8, 128), F32),
            V((LINE - 1, 4, 8, 128), F32),
            V((2, LINE - 1, 1, 8, 128), F32),
            V((LINE - 1, 4, 8, 128), F32),
            V((CLIPS, C), BF16),
            V((LINE, PLANE, CLIPS, EMB), BF16),
            V((CLIPS, C), F32),
            V((CLIPS, EMB), BF16),
            DMA((16,)),
            DMA((2, 3)),
            DMA((2, 3)),
            DMA((4,)),
            DMA((2,)),
            DMA((2, 3, 3)),
            DMA((2,)),
        ],
        compiler_params=pltpu.CompilerParams(
            collective_id=0, has_side_effects=True, vmem_limit_bytes=67043328
        ),
    )(
        clip_starts, key_feats, shuffle, query_feats, conv_time, conv_space, conv_expand,
        *rows, w_key, w_query, queue,
    )


def solution(mesh):
    placed = (
        (P(("dp", "bn"), None, None, None), P(("dp", "bn")), P("bn", None), P(("dp", "bn"), None)) + (P(),) * 12
    )
    return jax.shard_map(
        local, mesh=mesh, in_specs=placed, out_specs=(P(("dp", "bn"), None), P()), check_vma=False
    )
```

```python
import jax
import jax.numpy as jnp
from jax import lax
from jax.experimental import pallas as pl
from jax.experimental.pallas import tpu as pltpu
from jax.sharding import PartitionSpec as P

MESH = pl.DeviceIdType.MESH
F32, BF16, I32 = jnp.float32, jnp.bfloat16, jnp.int32
CLIPS, FRAMES, TF, SPOTS, SIDE = 8, 8, 12, 16, 4
C, INNER, EMB, QUEUE = 2048, 512, 128, 16384
PLANE, LINE, PEERS, ROUNDS = 16, 8, 32, 6
KC = 512
NK = C // KC
ROWS = CLIPS * FRAMES * SPOTS
COUNT = float(4 * ROWS)
EPS, TINY = 1e-05, 1e-06
PARTS = ((0, 640), (640, 640), (1280, 768))
ORDER = ((2, 1, 0), (1, 0, 2), (0, 2, 1))


def await_bytes(ref, sem):
    pltpu.make_async_copy(ref, ref, sem).wait()


def kernel(
    starts, feats, shuf, qf_h, wt_h, ws_h, we_h, g1, s1, g2, s2, g3, s3, wk_h, wq_h, queue_h,
    keys_out, qt_out, g_out,
    xall, xc, wt, acc, act, ws, act2, we, third, queue_v, qall, qt, wk, wq,
    tabv, tabs, picks, sb, ra, tb, rb, qmine, gall, pooled, gvec,
    hsem, asem, bsem, gsem, tsem, qsem, csem,
):
    i, x = lax.axis_index("dp"), lax.axis_index("bn")
    yz, core = i // 2, i % 2
    y, z = yz // 4, yz % 4
    xyz = (x, y, z)
    member = x * 2 + core
    half = core * 4 + x
    gall_plane = gall.at[0, pl.ds(0, PLANE - 1)]
    gall_line = gall.at[pl.ds(0, LINE - 1)]

    def plane_peer(k):
        return ((yz + k) % PLANE * 2 + core, x)

    def line_peer(k):
        m = (member + k) % LINE
        return (yz * 2 + m % 2, m // 2)

    def axis_peer(axis, k):
        c = list(xyz)
        c[axis] = (c[axis] + k) % 4
        return ((c[1] * 4 + c[2]) * 2 + core, c[0])

    barrier = pltpu.get_barrier_semaphore()
    for k in range(1, PLANE):
        pl.semaphore_signal(barrier, inc=1, device_id=plane_peer(k), device_id_type=MESH)
    for k in range(1, LINE):
        pl.semaphore_signal(barrier, inc=1, device_id=line_peer(k), device_id_type=MESH)

    def load(src, dst, n):
        return pltpu.make_async_copy(src, dst, hsem.at[n])

    own_q = qall.at[core, x, y, z]
    feat_loads = [load(feats.at[:, :, :, pl.ds(KC * k, KC)], xall[k], k) for k in range(NK)]
    wt_loads = [load(wt_h.at[:, pl.ds(KC * k, KC), :], wt.at[k], NK + k) for k in range(NK)]
    small = [load(qf_h, own_q, 8), load(qf_h, qmine, 9), load(wq_h, wq, 10)]
    queue_load = load(queue_h, queue_v, 11)
    ws_load = load(ws_h, ws, 12)
    we_loads = [load(we_h.at[:, pl.ds(INNER * q, INNER)], we.at[q], 16 + q) for q in range(4)]
    wk_load = load(wk_h, wk, 14)
    feat_loads[0].start()
    wt_loads[0].start()

    row = shuf[...].astype(F32)
    sq = (PEERS, PEERS)
    r_i = lax.broadcasted_iota(I32, sq, 0)
    c_i = lax.broadcasted_iota(I32, sq, 1)
    wide = jnp.broadcast_to(row, sq)
    column = jnp.sum(jnp.where(r_i == c_i, wide, 0.0), axis=1, keepdims=True)
    hit = column == c_i.astype(F32)
    inverse = jnp.sum(jnp.where(hit, r_i.astype(F32), 0.0), axis=0, keepdims=True)
    tabv[x] = jnp.zeros((8, 128), I32)
    tabv[4] = jnp.zeros((8, 128), I32)
    tabv[x, 0:1, 0:PEERS] = shuf[...]
    tabv[4, 0:1, 0:PEERS] = inverse.astype(I32)

    for k in range(NK):
        for e in (0, FRAMES + 1):
            xc[k, :, e] = jnp.zeros((CLIPS, SPOTS, KC), BF16)

    def conv_one(k):
        def pick(n, _):
            first = starts[n]
            for t in range(FRAMES):
                xc[k, n, 1 + t] = xall[k][n, first + t]
            return 0

        lax.fori_loop(0, CLIPS, pick, 0)

        def rows(p, _):
            lhs = jnp.concatenate(
                [xc[k, pl.ds(4 * p, 4), o : o + FRAMES].reshape(512, KC) for o in range(3)], axis=1
            )
            r = jnp.dot(lhs, wt[k].reshape(3 * KC, INNER), preferred_element_type=F32)
            at = pl.ds(pl.multiple_of(p * 512, 512), 512)
            for q in range(4):
                v = r[:, 128 * q : 128 * (q + 1)]
                acc[q, at, :] = v if k == 0 else acc[q, at, :] + v
            return 0

        lax.fori_loop(0, CLIPS // 4, rows, 0)

    def q_region(p, done):
        at = [pl.ds(xyz[a], 1) for a in range(3)]
        for a in done:
            at[a] = pl.ds(0, 4)
        return qall.at[(core, *at, slice(None), pl.ds(*PARTS[p]))]

    def q_send(phase):
        for p in range(3):
            part = q_region(p, ORDER[p][:phase])
            for k in range(1, 4):
                pltpu.make_async_remote_copy(
                    src_ref=part, dst_ref=part, send_sem=qsem.at[0, p, phase], recv_sem=qsem.at[1, p, phase],
                    device_id=axis_peer(ORDER[p][phase], k), device_id_type=MESH,
                ).start()

    def q_wait(phase, side):
        for p in range(3):
            cols = pl.ds(*PARTS[p])
            ref = (
                qall.at[0, 0, 0, pl.ds(0, 3), :, cols],
                qall.at[0, 0, pl.ds(0, 3), :, :, cols],
                qall.at[0, pl.ds(0, 3), :, :, :, cols],
            )[phase]
            await_bytes(ref, qsem.at[side, p, phase])

    core_copy = pltpu.make_async_remote_copy(
        src_ref=qall.at[core], dst_ref=qall.at[core], send_sem=csem.at[0], recv_sem=csem.at[1],
        device_id=(yz * 2 + 1 - core, x), device_id_type=MESH,
    )

    def plane_send(r):
        for k in range(1, PLANE):
            pltpu.make_async_remote_copy(
                src_ref=sb.at[r], dst_ref=ra[r].at[k - 1], send_sem=asem.at[0, r], recv_sem=asem.at[1, r],
                device_id=plane_peer(k), device_id_type=MESH,
            ).start()
        ra[r][PLANE - 1] = sb[r]

    def plane_forward(r):
        await_bytes(ra[r].at[pl.ds(0, PLANE - 1)], asem.at[1, r])
        for k in range(1, LINE):
            tb[r, k - 1] = ra[r][picks[0, k]] * jnp.where(picks[1, k] == 1, 1.0, 0.0).astype(F32)
            pltpu.make_async_remote_copy(
                src_ref=tb.at[r, k - 1], dst_ref=rb.at[r, k - 1], send_sem=bsem.at[0, r], recv_sem=bsem.at[1, r],
                device_id=line_peer(k), device_id_type=MESH,
            ).start()

    def line_finish(r):
        mine = ra[r][picks[0, 0]] * jnp.where(picks[1, 0] == 1, 1.0, 0.0).astype(F32)
        await_bytes(rb.at[r, pl.ds(0, LINE - 1)], bsem.at[1, r])
        for k in range(LINE - 1):
            mine = mine + rb[r, k]
        return mine

    def put_stats(r, parts):
        for q in range(4):
            sb[r, q : q + 1, :] = jnp.sum(parts[2 * q], axis=0, keepdims=True)
            sb[r, 4 + q : 5 + q, :] = jnp.sum(parts[2 * q + 1], axis=0, keepdims=True)

    def affine(tile, gain, shift):
        scales, shifts = [], []
        for q in range(4):
            m = tile[q : q + 1, :] * (1.0 / COUNT)
            w = tile[4 + q : 5 + q, :] * (1.0 / COUNT) - m * m
            scale = gain[:, 128 * q : 128 * (q + 1)] * lax.rsqrt(w + EPS)
            scales.append(scale)
            shifts.append(shift[:, 128 * q : 128 * (q + 1)] - m * scale)
        return jnp.concatenate(scales, axis=1), jnp.concatenate(shifts, axis=1)

    zeros = tuple(jnp.zeros((8, 128), F32) for _ in range(8))

    def sums_of(block):
        v = block.reshape(-1, 8, 128)
        return jnp.sum(v, axis=0), jnp.sum(v * v, axis=0)

    def rows_of(ref, at):
        return jnp.concatenate([ref[q, at, :] for q in range(4)], axis=1)

    def total_of(ref):
        def body(p, carry):
            out = list(carry)
            for q in range(4):
                a, b = sums_of(ref[q, pl.ds(pl.multiple_of(p * 128, 128), 128), :])
                out[2 * q] = out[2 * q] + a
                out[2 * q + 1] = out[2 * q + 1] + b
            return tuple(out)

        return lax.fori_loop(0, ROWS // 128, body, zeros)

    for k in range(NK):
        feat_loads[k].wait()
        wt_loads[k].wait()
        if k == 0:
            for d in small:
                d.start()
        if k + 1 < NK:
            feat_loads[k + 1].start()
            wt_loads[k + 1].start()
        if k == 2:
            queue_load.start()
            ws_load.start()
        if k == 3:
            for d in we_loads:
                d.start()
            wk_load.start()
        conv_one(k)
        if k == 0:
            pl.semaphore_wait(barrier, PLANE - 1 + LINE - 1)
            for d in small:
                d.wait()
            for n in range(1, 4):
                pltpu.make_async_remote_copy(
                    src_ref=tabv.at[x], dst_ref=tabv.at[x], send_sem=tsem.at[0], recv_sem=tsem.at[1],
                    device_id=axis_peer(0, n), device_id_type=MESH,
                ).start()
            q_send(0)
        if k == 2:
            q_wait(0, 1)
            q_send(1)
    put_stats(0, total_of(acc))
    plane_send(0)

    await_bytes(tabv.at[pl.ds(0, 3)], tsem.at[1])
    to_scalar = pltpu.make_async_copy(tabv, tabs, hsem.at[15])
    to_scalar.start()
    to_scalar.wait()
    for k in range(LINE):
        m = (member + k) % LINE
        group = tabs[m // 2, 0, yz * 2 + m % 2]
        j = tabs[4, 0, group]
        picks[0, k] = (yz - j // 2 + PLANE - 1) % PLANE
        picks[1, k] = jnp.where(j % 2 == core, 1, 0).astype(I32)

    zq = jnp.dot(qmine[...], wq[...], preferred_element_type=F32)
    length = jnp.sqrt(jnp.sum(zq * zq, axis=-1, keepdims=True) + TINY)
    unit = zq / length
    unit_b = unit.astype(BF16)
    queue_load.wait()

    def queue_part(lo, hi, carry):
        def body(n, carry):
            total, mix = carry
            qb = queue_v[pl.ds(pl.multiple_of(n * 1024, 1024), 1024), :].astype(F32)
            inv = lax.rsqrt(jnp.sum(qb * qb, axis=-1, keepdims=True) + TINY)
            qu = (qb * inv).astype(BF16)
            neg = lax.dot_general(unit_b, qu, (((1,), (1,)), ((), ())), preferred_element_type=F32) * 5.0
            e = jnp.exp(neg)
            total = total + jnp.sum(e, axis=-1, keepdims=True)
            mix = mix + jnp.dot(e.astype(BF16), qu, preferred_element_type=F32)
            return total, mix

        return lax.fori_loop(lo, hi, body, carry)

    carry = (jnp.zeros((CLIPS, 1), F32), jnp.zeros((CLIPS, EMB), F32))
    carry = queue_part(0, 8, carry)

    plane_forward(0)
    tile = line_finish(0)
    q_wait(1, 1)
    q_send(2)

    scale, shift = affine(tile, g1[...], s1[...])
    for r in range(4):
        for e in (0, SIDE + 1):
            act[r, e] = jnp.zeros((64, INNER), BF16)

    def norm_one(p, _):
        for r in range(SIDE):
            for c in range(SIDE):
                both = [
                    rows_of(acc, pl.ds((2 * p + h) * 128 + SIDE * r + c, FRAMES, stride=SPOTS)) for h in range(2)
                ]
                v = jnp.concatenate(both, axis=0)
                v = jnp.maximum(v * scale + shift, 0.0).astype(BF16)
                act[r, c + 1, pl.ds(pl.multiple_of(p * 16, 16), 16), :] = v
        return 0

    lax.fori_loop(0, CLIPS // 2, norm_one, 0)

    ws_load.wait()

    def row_conv(r, base, tap, taps):
        lhs = jnp.concatenate(
            [act[base + d, c : c + SIDE].reshape(256, INNER) for d in range(taps) for c in range(3)], axis=1
        )
        w = ws[pl.ds(tap, 3 * taps)].reshape(3 * taps * INNER, INNER)
        v = jnp.dot(lhs, w, preferred_element_type=F32)
        for q in range(4):
            acc[q, pl.ds(pl.multiple_of(r * 256, 256), 256), :] = v[:, 128 * q : 128 * (q + 1)]

    def edge(n, _):
        row_conv(3 * n, 2 * n, 3 - 3 * n, 2)
        return 0

    def middle(n, _):
        row_conv(1 + n, n, 0, 3)
        return 0

    lax.fori_loop(0, 2, edge, 0)
    lax.fori_loop(0, 2, middle, 0)
    put_stats(1, total_of(acc))
    plane_send(1)
    carry = queue_part(8, 16, carry)
    plane_forward(1)
    tile = line_finish(1)

    scale, shift = affine(tile, g2[...], s2[...])

    def norm_two(p, _):
        for h in range(8):
            v = rows_of(acc, pl.ds(p * 8 + h, SPOTS, stride=64))
            act2[pl.ds(pl.multiple_of(p * 128, 128) + h * 16, 16), :] = jnp.maximum(
                v * scale + shift, 0.0
            ).astype(BF16)
        return 0

    lax.fori_loop(0, CLIPS, norm_two, 0)
    for d in we_loads:
        d.wait()

    for q in range(4):

        def expand(p, carry):
            at = pl.ds(pl.multiple_of(p * 512, 512), 512)
            v = jnp.dot(act2[at, :], we[q], preferred_element_type=F32)
            third[q, at, :] = v
            out = list(carry)
            for c in range(4):
                a, b = sums_of(v[:, 128 * c : 128 * (c + 1)])
                out[2 * c] = out[2 * c] + a
                out[2 * c + 1] = out[2 * c + 1] + b
            return tuple(out)

        put_stats(2 + q, lax.fori_loop(0, 2, expand, zeros))
        plane_send(2 + q)
    q_wait(2, 1)
    core_copy.start()
    for q in range(4):
        plane_forward(2 + q)

    for q in range(4):
        cols = slice(INNER * q, INNER * (q + 1))
        scale, shift = affine(line_finish(2 + q), g3[:, cols], s3[:, cols])

        def pool(n, _):
            at = pl.ds(pl.multiple_of(n * 128, 128), 128)
            for c in range(4):
                lanes = slice(128 * c, 128 * (c + 1))
                kept = xc[q, n, 1 : 1 + FRAMES, :, lanes].reshape(128, 128).astype(F32)
                v = jnp.maximum(third[q, at, lanes] * scale[:, lanes] + shift[:, lanes] + kept, 0.0)
                pooled[n, :, INNER * q + 128 * c : INNER * q + 128 * (c + 1)] = jnp.sum(
                    v.reshape(16, 8, 128), axis=0
                )
            return 0

        lax.fori_loop(0, CLIPS, pool, 0)
    wk_load.wait()
    mean = jnp.sum(pooled[...], axis=1) * (1.0 / 128.0)
    projected = jnp.dot(mean.astype(BF16), wk[...], preferred_element_type=F32)
    norm = jnp.sum(projected * projected, axis=-1, keepdims=True) + TINY
    keys = (projected * lax.rsqrt(norm)).astype(BF16)
    keys_out[...] = keys

    held = keys.astype(F32)
    total, mix = carry
    e_pos = jnp.exp(jnp.sum(unit * held, axis=-1, keepdims=True) * 5.0)
    whole = e_pos + total
    grad = (mix / whole + (e_pos / whole - 1.0) * held) * 5.0
    radial = jnp.sum(unit * grad, axis=-1, keepdims=True)
    gvec[...] = ((grad - radial * unit) / length).astype(BF16)
    for k in range(1, PLANE):
        pltpu.make_async_remote_copy(
            src_ref=gvec, dst_ref=gall.at[half, yz], send_sem=gsem.at[0], recv_sem=gsem.at[1],
            device_id=plane_peer(k), device_id_type=MESH,
        ).start()
    gall[half, yz] = gvec[...]
    core_copy.wait_recv()

    def turn(n, _):
        cols = pl.ds(pl.multiple_of(n * 128, 128), 128)
        v = qall[:, :, :, :, :, cols].astype(F32).reshape(1024, 128)
        qt[cols, :] = v.T.astype(BF16)
        return 0

    lax.fori_loop(0, C // 128, turn, 0)
    qt_store = load(qt, qt_out, 15)
    qt_store.start()
    await_bytes(gall_plane, gsem.at[1])
    own_half = pltpu.make_async_copy(gall.at[half], g_out.at[half], hsem.at[13])
    own_half.start()
    for k in range(1, LINE):
        pltpu.make_async_remote_copy(
            src_ref=gall.at[half], dst_ref=g_out.at[half], send_sem=gsem.at[2], recv_sem=gsem.at[3],
            device_id=line_peer(k), device_id_type=MESH,
        ).start()
    await_bytes(gall_line, gsem.at[3])
    own_half.wait()
    qt_store.wait()

    await_bytes(tabv.at[pl.ds(0, 3)], tsem.at[0])
    for phase in range(3):
        q_wait(phase, 0)
    core_copy.wait_send()
    for r in range(ROUNDS):
        await_bytes(ra[r].at[pl.ds(0, PLANE - 1)], asem.at[0, r])
        await_bytes(rb.at[r, pl.ds(0, LINE - 1)], bsem.at[0, r])
    await_bytes(gall_plane, gsem.at[0])
    await_bytes(gall_line, gsem.at[2])


def last(keys_ref, q_ref, g_ref, keys_out, grad_out):
    keys_out[...] = keys_ref[...]
    grad_out[...] = jnp.dot(q_ref[...], g_ref[...], preferred_element_type=F32)


def local(
    key_feats, clip_starts, shuffle, query_feats, conv_time, conv_space, conv_expand,
    gain_one, shift_one, gain_two, shift_two, gain_three, shift_three, w_key, w_query, queue,
):
    vmem = pl.BlockSpec(memory_space=pltpu.VMEM)
    smem = pl.BlockSpec(memory_space=pltpu.SMEM)
    hbm = pl.BlockSpec(memory_space=pltpu.HBM)
    V = pltpu.VMEM
    DMA = pltpu.SemaphoreType.DMA
    rows = [v.reshape(1, -1) for v in (gain_one, shift_one, gain_two, shift_two, gain_three, shift_three)]
    keys, q_t, grads = pl.pallas_call(
        kernel,
        name="moco",
        out_shape=(
            jax.ShapeDtypeStruct((CLIPS, EMB), BF16),
            jax.ShapeDtypeStruct((C, 1024), BF16),
            jax.ShapeDtypeStruct((LINE, PLANE, CLIPS, EMB), BF16),
        ),
        in_specs=[smem, hbm, vmem, hbm, hbm, hbm, hbm] + [vmem] * 6 + [hbm] * 3,
        out_specs=(vmem, hbm, hbm),
        scratch_shapes=[
            [V((CLIPS, TF, SPOTS, KC), BF16) for _ in range(NK)],
            V((NK, CLIPS, FRAMES + 2, SPOTS, KC), BF16),
            V((NK, 3, KC, INNER), BF16),
            V((4, ROWS, 128), F32),
            V((SIDE, SIDE + 2, 64, INNER), BF16),
            V((9, INNER, INNER), BF16),
            V((ROWS, INNER), BF16),
            V((4, INNER, INNER), BF16),
            V((4, ROWS, INNER), F32),
            V((QUEUE, EMB), BF16),
            V((2, 4, 4, 4, CLIPS, C), BF16),
            V((C, 1024), BF16),
            V((C, EMB), BF16),
            V((C, EMB), BF16),
            V((5, 8, 128), I32),
            pltpu.SMEM((5, 8, 128), I32),
            pltpu.SMEM((2, LINE), I32),
            V((ROUNDS, 8, 128), F32),
            [V((PLANE, 8, 128), F32) for _ in range(ROUNDS)],
            V((ROUNDS, LINE - 1, 8, 128), F32),
            V((ROUNDS, LINE - 1, 8, 128), F32),
            V((CLIPS, C), BF16),
            V((LINE, PLANE, CLIPS, EMB), BF16),
            V((CLIPS, 8, C), F32),
            V((CLIPS, EMB), BF16),
            DMA((20,)),
            DMA((2, ROUNDS)),
            DMA((2, ROUNDS)),
            DMA((4,)),
            DMA((2,)),
            DMA((2, 3, 3)),
            DMA((2,)),
        ],
        compiler_params=pltpu.CompilerParams(
            collective_id=0, has_side_effects=True, vmem_limit_bytes=67043328
        ),
    )(
        clip_starts, key_feats, shuffle, query_feats, conv_time, conv_space, conv_expand,
        *rows, w_key, w_query, queue,
    )
    tall = C // 4
    return pl.pallas_call(
        last,
        name="last",
        grid=(4,),
        out_shape=(jax.ShapeDtypeStruct((CLIPS, EMB), BF16), jax.ShapeDtypeStruct((C, EMB), F32)),
        in_specs=[
            pl.BlockSpec((CLIPS, EMB), lambda n: (0, 0)),
            pl.BlockSpec((tall, 1024), lambda n: (n, 0)),
            pl.BlockSpec((1024, EMB), lambda n: (0, 0)),
        ],
        out_specs=(pl.BlockSpec((CLIPS, EMB), lambda n: (0, 0)), pl.BlockSpec((tall, EMB), lambda n: (n, 0))),
    )(keys, q_t, grads.reshape(1024, EMB))


def solution(mesh):
    placed = (
        (P(("dp", "bn"), None, None, None), P(("dp", "bn")), P("bn", None), P(("dp", "bn"), None)) + (P(),) * 12
    )
    return jax.shard_map(
        local, mesh=mesh, in_specs=placed, out_specs=(P(("dp", "bn"), None), P()), check_vma=False
    )
```

```python
import jax
import jax.numpy as jnp
from jax import lax
from jax.experimental import pallas as pl
from jax.experimental.pallas import tpu as pltpu
from jax.sharding import PartitionSpec as P

MESH = pl.DeviceIdType.MESH
F32, BF16, I32 = jnp.float32, jnp.bfloat16, jnp.int32
CLIPS, FRAMES, TF, SPOTS, SIDE = 8, 8, 12, 16, 4
C, INNER, EMB, QUEUE = 2048, 512, 128, 16384
PLANE, LINE, PEERS, ROUNDS, PIECES = 16, 8, 32, 6, 4
KC = 512
NK = C // KC
ROWS = CLIPS * FRAMES * SPOTS
COUNT = float(4 * ROWS)
EPS, TINY = 1e-05, 1e-06
PARTS = ((0, 640), (640, 640), (1280, 768))
ORDER = ((2, 1, 0), (1, 0, 2), (0, 2, 1))


def await_bytes(ref, sem):
    pltpu.make_async_copy(ref, ref, sem).wait()


def kernel(
    starts_h, feats, shuf_h, qf_h, wt_h, ws_h, we_h, g1_h, s1_h, g2_h, s2_h, g3_h, s3_h, wk_h, wq_h, queue_h,
    keys_out, qt_out, g_out,
    xall, wt, acc, act, ws, act2, we, third, queue_v, qall, qt, wk, wq,
    tabv, tabs, picks, sb, ra, tb, rb, qmine, gall, pooled, gvec, keys_v,
    starts, shuf, g1, s1, g2, s2, g3, s3,
    hsem, asem, bsem, gsem, tsem, qsem, csem,
):
    i, x = lax.axis_index("dp"), lax.axis_index("bn")
    yz, core = i // 2, i % 2
    y, z = yz // 4, yz % 4
    xyz = (x, y, z)
    member = x * 2 + core
    half = core * 4 + x
    gall_plane = gall.at[0, pl.ds(0, PLANE - 1)]
    gall_line = gall.at[pl.ds(0, LINE - 1)]

    def plane_peer(k):
        return ((yz + k) % PLANE * 2 + core, x)

    def line_peer(k):
        m = (member + k) % LINE
        return (yz * 2 + m % 2, m // 2)

    def axis_peer(axis, k):
        c = list(xyz)
        c[axis] = (c[axis] + k) % 4
        return ((c[1] * 4 + c[2]) * 2 + core, c[0])

    def load(src, dst, n):
        return pltpu.make_async_copy(src, dst, hsem.at[n])

    own_q = qall.at[core, x, y, z]
    feat_loads = [load(feats.at[:, :, :, pl.ds(KC * k, KC)], xall[k], k) for k in range(NK)]
    wt_loads = [load(wt_h.at[:, pl.ds(KC * k, KC), :], wt.at[k], NK + k) for k in range(NK)]
    small = [load(a, b, 22 + n) for n, (a, b) in enumerate(zip((g1_h, s1_h, g2_h, s2_h, g3_h, s3_h), (g1, s1, g2, s2, g3, s3)))]
    small += [load(qf_h, own_q, 8), load(qf_h, qmine, 9), load(wq_h, wq, 10)]
    queue_load = load(queue_h, queue_v, 11)
    ws_load = load(ws_h, ws, 12)
    we_loads = [load(we_h.at[:, pl.ds(INNER * q, INNER)], we.at[q], 16 + q) for q in range(4)]
    wk_load = load(wk_h, wk, 14)
    feat_loads[0].start()
    wt_loads[0].start()
    first_loads = [load(starts_h, starts, 20), load(shuf_h, shuf, 21)]
    for d in first_loads:
        d.start()
    barrier = pltpu.get_barrier_semaphore()
    for k in range(1, PLANE):
        pl.semaphore_signal(barrier, inc=1, device_id=plane_peer(k), device_id_type=MESH)
    for k in range(1, LINE):
        pl.semaphore_signal(barrier, inc=1, device_id=line_peer(k), device_id_type=MESH)


    for d in first_loads:
        d.wait()
    row = shuf[...].astype(F32)
    sq = (PEERS, PEERS)
    r_i = lax.broadcasted_iota(I32, sq, 0)
    c_i = lax.broadcasted_iota(I32, sq, 1)
    wide = jnp.broadcast_to(row, sq)
    column = jnp.sum(jnp.where(r_i == c_i, wide, 0.0), axis=1, keepdims=True)
    hit = column == c_i.astype(F32)
    inverse = jnp.sum(jnp.where(hit, r_i.astype(F32), 0.0), axis=0, keepdims=True)
    tabv[x] = jnp.zeros((8, 128), I32)
    tabv[4] = jnp.zeros((8, 128), I32)
    tabv[x, 0:1, 0:PEERS] = shuf[...]
    tabv[4, 0:1, 0:PEERS] = inverse.astype(I32)

    def conv_one(k):
        empty = jnp.zeros((SPOTS, KC), BF16)

        def rows(p, _):
            taps = []
            for o in range(3):
                blocks = []
                for m in range(4):
                    n = p * 4 + m
                    first = starts[n] + (o - 1)
                    for t in range(FRAMES):
                        inside = 0 <= t + o - 1 < FRAMES
                        blocks.append(xall[k][n, first + t] if inside else empty)
                taps.append(jnp.concatenate(blocks, axis=0))
            lhs = jnp.concatenate(taps, axis=1)
            r = jnp.dot(lhs, wt[k].reshape(3 * KC, INNER), preferred_element_type=F32)
            at = pl.ds(pl.multiple_of(p * 512, 512), 512)
            for q in range(4):
                v = r[:, 128 * q : 128 * (q + 1)]
                acc[q, at, :] = v if k == 0 else acc[q, at, :] + v
            return 0

        lax.fori_loop(0, CLIPS // 4, rows, 0)

    def q_region(p, phase):
        at = [pl.ds(xyz[a], 1) for a in range(3)]
        if phase >= 1:
            at[ORDER[p][0]] = pl.ds(0, 4)
        if phase >= 2:
            at[ORDER[p][0]] = pl.ds(2 * (phase - 2), 2)
            at[ORDER[p][1]] = pl.ds(0, 4)
        return qall.at[(core, *at, slice(None), pl.ds(*PARTS[p]))]

    def q_send(phase, parts=(0, 1, 2)):
        for p in parts:
            part = q_region(p, phase)
            for k in range(1, 4):
                pltpu.make_async_remote_copy(
                    src_ref=part, dst_ref=part, send_sem=qsem.at[0, p, phase], recv_sem=qsem.at[1, p, phase],
                    device_id=axis_peer(ORDER[p][min(phase, 2)], k), device_id_type=MESH,
                ).start()

    def q_wait(phase, side, parts=(0, 1, 2)):
        for p in parts:
            cols = pl.ds(*PARTS[p])
            half_phase = qall.at[0, pl.ds(0, 3), pl.ds(0, 2), :, :, cols]
            ref = (
                qall.at[0, 0, 0, pl.ds(0, 3), :, cols],
                qall.at[0, 0, pl.ds(0, 3), :, :, cols],
                half_phase,
                half_phase,
            )[phase]
            await_bytes(ref, qsem.at[side, p, phase])

    core_copy = pltpu.make_async_remote_copy(
        src_ref=qall.at[core], dst_ref=qall.at[core], send_sem=csem.at[0], recv_sem=csem.at[1],
        device_id=(yz * 2 + 1 - core, x), device_id_type=MESH,
    )

    def plane_send(r):
        for k in range(1, PLANE):
            pltpu.make_async_remote_copy(
                src_ref=sb.at[r], dst_ref=ra[r].at[k - 1], send_sem=asem.at[0, r], recv_sem=asem.at[1, r],
                device_id=plane_peer(k), device_id_type=MESH,
            ).start()
        ra[r][PLANE - 1] = sb[r]

    def plane_forward(r):
        await_bytes(ra[r].at[pl.ds(0, PLANE - 1)], asem.at[1, r])
        for k in range(1, LINE):
            tb[r, k - 1] = ra[r][picks[0, k]] * jnp.where(picks[1, k] == 1, 1.0, 0.0).astype(F32)
            pltpu.make_async_remote_copy(
                src_ref=tb.at[r, k - 1], dst_ref=rb.at[r, k - 1], send_sem=bsem.at[0, r], recv_sem=bsem.at[1, r],
                device_id=line_peer(k), device_id_type=MESH,
            ).start()

    def line_finish(r):
        mine = ra[r][picks[0, 0]] * jnp.where(picks[1, 0] == 1, 1.0, 0.0).astype(F32)
        await_bytes(rb.at[r, pl.ds(0, LINE - 1)], bsem.at[1, r])
        for k in range(LINE - 1):
            mine = mine + rb[r, k]
        return mine

    def put_stats(r, parts):
        for q in range(4):
            sb[r, q : q + 1, :] = jnp.sum(parts[2 * q], axis=0, keepdims=True)
            sb[r, 4 + q : 5 + q, :] = jnp.sum(parts[2 * q + 1], axis=0, keepdims=True)

    def affine(tile, gain, shift):
        scales, shifts = [], []
        for q in range(4):
            m = tile[q : q + 1, :] * (1.0 / COUNT)
            w = tile[4 + q : 5 + q, :] * (1.0 / COUNT) - m * m
            scale = gain[:, 128 * q : 128 * (q + 1)] * lax.rsqrt(w + EPS)
            scales.append(scale)
            shifts.append(shift[:, 128 * q : 128 * (q + 1)] - m * scale)
        return jnp.concatenate(scales, axis=1), jnp.concatenate(shifts, axis=1)

    zeros = tuple(jnp.zeros((8, 128), F32) for _ in range(8))

    def sums_of(block):
        v = block.reshape(-1, 8, 128)
        return jnp.sum(v, axis=0), jnp.sum(v * v, axis=0)

    def rows_of(ref, at):
        return jnp.concatenate([ref[q, at, :] for q in range(4)], axis=1)

    def total_of(ref):
        def body(p, carry):
            out = list(carry)
            for q in range(4):
                a, b = sums_of(ref[q, pl.ds(pl.multiple_of(p * 128, 128), 128), :])
                out[2 * q] = out[2 * q] + a
                out[2 * q + 1] = out[2 * q + 1] + b
            return tuple(out)

        return lax.fori_loop(0, ROWS // 128, body, zeros)

    to_scalar = pltpu.make_async_copy(tabv, tabs, hsem.at[15])

    def find_picks():
        to_scalar.wait()
        for k in range(LINE):
            m = (member + k) % LINE
            group = tabs[m // 2, 0, yz * 2 + m % 2]
            j = tabs[4, 0, group]
            picks[0, k] = (yz - j // 2 + PLANE - 1) % PLANE
            picks[1, k] = jnp.where(j % 2 == core, 1, 0).astype(I32)

    for k in range(NK):
        feat_loads[k].wait()
        wt_loads[k].wait()
        if k == 0:
            for d in small:
                d.start()
        if k + 1 < NK:
            feat_loads[k + 1].start()
            wt_loads[k + 1].start()
        if k == 2:
            queue_load.start()
            ws_load.start()
        if k == 3:
            for d in we_loads:
                d.start()
            wk_load.start()
        conv_one(k)
        if k == 0:
            pl.semaphore_wait(barrier, PLANE - 1 + LINE - 1)
            for d in small:
                d.wait()
            for n in range(1, 4):
                pltpu.make_async_remote_copy(
                    src_ref=tabv.at[x], dst_ref=tabv.at[x], send_sem=tsem.at[0], recv_sem=tsem.at[1],
                    device_id=axis_peer(0, n), device_id_type=MESH,
                ).start()
            q_send(0)
        if k == 2:
            q_wait(0, 1)
            q_send(1)
            await_bytes(tabv.at[pl.ds(0, 3)], tsem.at[1])
            to_scalar.start()
        if k == 3:
            find_picks()
    put_stats(0, total_of(acc))
    plane_send(0)

    zq = jnp.dot(qmine[...], wq[...], preferred_element_type=F32)
    length = jnp.sqrt(jnp.sum(zq * zq, axis=-1, keepdims=True) + TINY)
    unit = zq / length
    unit_b = unit.astype(BF16)
    queue_load.wait()

    def queue_part(lo, hi, carry):
        def body(n, carry):
            total, mix = carry
            qb = queue_v[pl.ds(pl.multiple_of(n * 1024, 1024), 1024), :].astype(F32)
            inv = lax.rsqrt(jnp.sum(qb * qb, axis=-1, keepdims=True) + TINY)
            qu = (qb * inv).astype(BF16)
            neg = lax.dot_general(unit_b, qu, (((1,), (1,)), ((), ())), preferred_element_type=F32) * 5.0
            e = jnp.exp(neg)
            total = total + jnp.sum(e, axis=-1, keepdims=True)
            mix = mix + jnp.dot(e.astype(BF16), qu, preferred_element_type=F32)
            return total, mix

        return lax.fori_loop(lo, hi, body, carry)

    carry = (jnp.zeros((CLIPS, 1), F32), jnp.zeros((CLIPS, EMB), F32))
    carry = queue_part(0, 6, carry)

    plane_forward(0)
    q_wait(1, 1)
    q_send(2, (1, 2))
    carry = queue_part(6, 9, carry)
    tile = line_finish(0)
    q_send(2, (0,))
    q_send(3, (1, 2))

    scale, shift = affine(tile, g1[...], s1[...])
    for r in range(4):
        for e in (0, SIDE + 1):
            act[r, e] = jnp.zeros((64, INNER), BF16)

    def norm_one(p, _):
        for r in range(SIDE):
            for c in range(SIDE):
                both = [
                    rows_of(acc, pl.ds((2 * p + h) * 128 + SIDE * r + c, FRAMES, stride=SPOTS)) for h in range(2)
                ]
                v = jnp.concatenate(both, axis=0)
                v = jnp.maximum(v * scale + shift, 0.0).astype(BF16)
                act[r, c + 1, pl.ds(pl.multiple_of(p * 16, 16), 16), :] = v
        return 0

    lax.fori_loop(0, CLIPS // 2, norm_one, 0)

    ws_load.wait()

    def row_conv(r, base, tap, taps):
        lhs = jnp.concatenate(
            [act[base + d, c : c + SIDE].reshape(256, INNER) for d in range(taps) for c in range(3)], axis=1
        )
        w = ws[pl.ds(tap, 3 * taps)].reshape(3 * taps * INNER, INNER)
        v = jnp.dot(lhs, w, preferred_element_type=F32)
        for q in range(4):
            acc[q, pl.ds(pl.multiple_of(r * 256, 256), 256), :] = v[:, 128 * q : 128 * (q + 1)]

    def edge(n, _):
        row_conv(3 * n, 2 * n, 3 - 3 * n, 2)
        return 0

    def middle(n, _):
        row_conv(1 + n, n, 0, 3)
        return 0

    lax.fori_loop(0, 2, edge, 0)
    lax.fori_loop(0, 2, middle, 0)
    put_stats(1, total_of(acc))
    plane_send(1)
    q_send(3, (0,))
    carry = queue_part(9, 15, carry)
    plane_forward(1)
    carry = queue_part(15, 16, carry)
    tile = line_finish(1)
    q_wait(2, 1)
    q_wait(3, 1)
    core_copy.start()

    scale, shift = affine(tile, g2[...], s2[...])

    side = (128, 128)
    to = lax.broadcasted_iota(I32, side, 0)
    source = lax.broadcasted_iota(I32, side, 1)
    swap = jnp.where((to % 16) * 8 + to // 16 == source, 1.0, 0.0).astype(BF16)

    def norm_two(p, _):
        for n in (2 * p, 2 * p + 1):
            chunks = []
            for q in range(4):
                lanes = slice(128 * q, 128 * (q + 1))
                rows = [acc[q, pl.ds(pl.multiple_of(n * 8, 8) + 64 * s, 8), :] for s in range(SPOTS)]
                v = jnp.concatenate(rows, axis=0) * scale[:, lanes] + shift[:, lanes]
                chunks.append(jnp.maximum(v, 0.0).astype(BF16))
            v = jnp.dot(swap, jnp.concatenate(chunks, axis=1), preferred_element_type=F32)
            act2[pl.ds(pl.multiple_of(n * 128, 128), 128), :] = v.astype(BF16)
        return 0

    lax.fori_loop(0, CLIPS // 2, norm_two, 0)
    for d in we_loads:
        d.wait()

    for q in range(4):

        sums = list(zeros)
        for p in range(2):
            at = pl.ds(p * 512, 512)
            v = jnp.dot(act2[at, :], we[q], preferred_element_type=F32)
            third[q, at, :] = v
            for c in range(4):
                a, b = sums_of(v[:, 128 * c : 128 * (c + 1)])
                sums[2 * c] = sums[2 * c] + a
                sums[2 * c + 1] = sums[2 * c + 1] + b
        put_stats(2 + q, sums)
        plane_send(2 + q)
    for q in range(4):
        plane_forward(2 + q)

    for q in range(4):
        cols = slice(INNER * q, INNER * (q + 1))
        scale, shift = affine(line_finish(2 + q), g3[:, cols], s3[:, cols])

        def pool(n, _):
            at = pl.ds(pl.multiple_of(n * 128, 128), 128)
            first = starts[n]
            for c in range(4):
                lanes = slice(128 * c, 128 * (c + 1))
                kept = jnp.concatenate([xall[q][n, first + t, :, lanes] for t in range(FRAMES)], axis=0).astype(F32)
                v = jnp.maximum(third[q, at, lanes] * scale[:, lanes] + shift[:, lanes] + kept, 0.0)
                pooled[n, :, INNER * q + 128 * c : INNER * q + 128 * (c + 1)] = jnp.sum(
                    v.reshape(16, 8, 128), axis=0
                )
            return 0

        lax.fori_loop(0, CLIPS, pool, 0)
    wk_load.wait()
    mean = jnp.sum(pooled[...], axis=1) * (1.0 / 128.0)
    projected = jnp.dot(mean.astype(BF16), wk[...], preferred_element_type=F32)
    norm = jnp.sum(projected * projected, axis=-1, keepdims=True) + TINY
    keys = (projected * lax.rsqrt(norm)).astype(BF16)
    keys_v[...] = keys
    keys_store = load(keys_v, keys_out, 12)
    keys_store.start()

    held = keys.astype(F32)
    total, mix = carry
    e_pos = jnp.exp(jnp.sum(unit * held, axis=-1, keepdims=True) * 5.0)
    whole = e_pos + total
    grad = (mix / whole + (e_pos / whole - 1.0) * held) * 5.0
    radial = jnp.sum(unit * grad, axis=-1, keepdims=True)
    gvec[...] = ((grad - radial * unit) / length).astype(BF16)
    for k in range(1, PLANE):
        pltpu.make_async_remote_copy(
            src_ref=gvec, dst_ref=gall.at[half, yz], send_sem=gsem.at[0], recv_sem=gsem.at[1],
            device_id=plane_peer(k), device_id_type=MESH,
        ).start()
    gall[half, yz] = gvec[...]
    core_copy.wait_recv()

    def turn(n, _):
        cols = pl.ds(pl.multiple_of(n * 128, 128), 128)
        v = qall[:, :, :, :, :, cols].astype(F32).reshape(1024, 128)
        qt[cols, :] = v.T.astype(BF16)
        return 0

    lax.fori_loop(0, C // 128, turn, 0)
    qt_store = load(qt, qt_out, 15)
    qt_store.start()
    await_bytes(gall_plane, gsem.at[1])
    own_half = pltpu.make_async_copy(gall.at[half], g_out.at[half], hsem.at[13])
    own_half.start()
    for k in range(1, LINE):
        pltpu.make_async_remote_copy(
            src_ref=gall.at[half], dst_ref=g_out.at[half], send_sem=gsem.at[2], recv_sem=gsem.at[3],
            device_id=line_peer(k), device_id_type=MESH,
        ).start()
    await_bytes(gall_line, gsem.at[3])
    own_half.wait()
    qt_store.wait()
    keys_store.wait()

    await_bytes(tabv.at[pl.ds(0, 3)], tsem.at[0])
    for phase in range(4):
        q_wait(phase, 0)
    core_copy.wait_send()
    for r in range(ROUNDS):
        await_bytes(ra[r].at[pl.ds(0, PLANE - 1)], asem.at[0, r])
        await_bytes(rb.at[r, pl.ds(0, LINE - 1)], bsem.at[0, r])
    await_bytes(gall_plane, gsem.at[0])
    await_bytes(gall_line, gsem.at[2])


def last(keys_ref, q_ref, g_ref, keys_out, grad_out, keys_v, q_v, g_v, out_v, sem):
    tall = C // PIECES

    def rows(n):
        return pl.ds(n * tall, tall)

    keys_in = pltpu.make_async_copy(keys_ref, keys_v, sem.at[0])
    g_in = pltpu.make_async_copy(g_ref, g_v, sem.at[1])
    q_in = [pltpu.make_async_copy(q_ref.at[rows(n)], q_v.at[n], sem.at[2 + n]) for n in range(PIECES)]
    g_in.start()
    for d in q_in:
        d.start()
    keys_in.start()
    stores = []
    g_in.wait()
    for n in range(PIECES):
        q_in[n].wait()
        out_v[n] = jnp.dot(q_v[n], g_v[...], preferred_element_type=F32)
        d = pltpu.make_async_copy(out_v.at[n], grad_out.at[rows(n)], sem.at[2 + PIECES + n])
        d.start()
        stores.append(d)
    keys_in.wait()
    d = pltpu.make_async_copy(keys_v, keys_out, sem.at[0])
    d.start()
    for e in stores:
        e.wait()
    d.wait()


def local(
    key_feats, clip_starts, shuffle, query_feats, conv_time, conv_space, conv_expand,
    gain_one, shift_one, gain_two, shift_two, gain_three, shift_three, w_key, w_query, queue,
):
    hbm = pl.BlockSpec(memory_space=pltpu.HBM)
    V = pltpu.VMEM
    DMA = pltpu.SemaphoreType.DMA
    rows = [v.reshape(1, -1) for v in (gain_one, shift_one, gain_two, shift_two, gain_three, shift_three)]
    keys, q_t, grads = pl.pallas_call(
        kernel,
        name="moco",
        out_shape=(
            jax.ShapeDtypeStruct((CLIPS, EMB), BF16),
            jax.ShapeDtypeStruct((C, 1024), BF16),
            jax.ShapeDtypeStruct((LINE, PLANE, CLIPS, EMB), BF16),
        ),
        in_specs=[hbm] * 16,
        out_specs=(hbm, hbm, hbm),
        scratch_shapes=[
            [V((CLIPS, TF, SPOTS, KC), BF16) for _ in range(NK)],
            V((NK, 3, KC, INNER), BF16),
            V((4, ROWS, 128), F32),
            V((SIDE, SIDE + 2, 64, INNER), BF16),
            V((9, INNER, INNER), BF16),
            V((ROWS, INNER), BF16),
            V((4, INNER, INNER), BF16),
            V((4, ROWS, INNER), F32),
            V((QUEUE, EMB), BF16),
            V((2, 4, 4, 4, CLIPS, C), BF16),
            V((C, 1024), BF16),
            V((C, EMB), BF16),
            V((C, EMB), BF16),
            V((5, 8, 128), I32),
            pltpu.SMEM((5, 8, 128), I32),
            pltpu.SMEM((2, LINE), I32),
            V((ROUNDS, 8, 128), F32),
            [V((PLANE, 8, 128), F32) for _ in range(ROUNDS)],
            V((ROUNDS, LINE - 1, 8, 128), F32),
            V((ROUNDS, LINE - 1, 8, 128), F32),
            V((CLIPS, C), BF16),
            V((LINE, PLANE, CLIPS, EMB), BF16),
            V((CLIPS, 8, C), F32),
            V((CLIPS, EMB), BF16),
            V((CLIPS, EMB), BF16),
            pltpu.SMEM((CLIPS,), I32),
            V((1, PEERS), I32),
            *[V((1, n), F32) for n in (INNER,) * 4 + (C,) * 2],
            DMA((30,)),
            DMA((2, ROUNDS)),
            DMA((2, ROUNDS)),
            DMA((4,)),
            DMA((2,)),
            DMA((2, 3, 4)),
            DMA((2,)),
        ],
        compiler_params=pltpu.CompilerParams(
            collective_id=0, has_side_effects=True, vmem_limit_bytes=67043328
        ),
    )(
        clip_starts, key_feats, shuffle, query_feats, conv_time, conv_space, conv_expand,
        *rows, w_key, w_query, queue,
    )
    return pl.pallas_call(
        last,
        name="last",
        out_shape=(jax.ShapeDtypeStruct((CLIPS, EMB), BF16), jax.ShapeDtypeStruct((C, EMB), F32)),
        in_specs=[hbm] * 3,
        out_specs=(hbm, hbm),
        scratch_shapes=[
            V((CLIPS, EMB), BF16),
            V((PIECES, C // PIECES, 1024), BF16),
            V((1024, EMB), BF16),
            V((PIECES, C // PIECES, EMB), F32),
            DMA((2 + 2 * PIECES,)),
        ],
    )(keys, q_t, grads.reshape(1024, EMB))


def solution(mesh):
    placed = (
        (P(("dp", "bn"), None, None, None), P(("dp", "bn")), P("bn", None), P(("dp", "bn"), None)) + (P(),) * 12
    )
    return jax.shard_map(
        local, mesh=mesh, in_specs=placed, out_specs=(P(("dp", "bn"), None), P()), check_vma=False
    )
```

```python
import jax
import jax.numpy as jnp
from jax import lax
from jax.experimental import pallas as pl
from jax.experimental.pallas import tpu as pltpu
from jax.sharding import PartitionSpec as P

MESH = pl.DeviceIdType.MESH
F32, BF16, I32 = jnp.float32, jnp.bfloat16, jnp.int32
CLIPS, FRAMES, TF, SPOTS, SIDE, CHIPS = 8, 8, 12, 16, 4, 64
C, INNER, EMB, QUEUE = 2048, 512, 128, 16384
PLANE, LINE, PEERS, ROUNDS, PIECES = 16, 8, 32, 7, 8
KC = 512
NK = C // KC
ROWS = CLIPS * FRAMES * SPOTS
COUNT = float(4 * ROWS)
EPS, TINY = 1e-05, 1e-06
PARTS = ((0, 640), (640, 640), (1280, 768))
ORDER = ((2, 1, 0), (1, 0, 2), (0, 2, 1))


def await_bytes(ref, sem):
    pltpu.make_async_copy(ref, ref, sem).wait()


def kernel(
    starts_h, feats, shuf_h, qf_h, wt_h, ws_h, we_h, g1_h, s1_h, g2_h, s2_h, g3_h, s3_h, wk_h, wq_h, queue_h,
    keys_out, qt_out, g_out,
    xall, wt, acc, second, act, ws, act2, we, third, queue_v, qall, qt, wk, wq,
    tabv, tabs, picks, sb, ra, tb, rb, qmine, gall, pooled, gvec, keys_v,
    starts, shuf, g1, s1, g2, s2, g3, s3,
    hsem, asem, bsem, gsem, tsem, qsem, csem,
):
    i, x = lax.axis_index("dp"), lax.axis_index("bn")
    yz, core = i // 2, i % 2
    y, z = yz // 4, yz % 4
    xyz = (x, y, z)
    member = x * 2 + core
    chip = x * 16 + yz

    def plane_peer(k):
        return ((yz + k) % PLANE * 2 + core, x)

    def line_peer(k):
        m = (member + k) % LINE
        return (yz * 2 + m % 2, m // 2)

    def chip_peer(k):
        c = (x + k // 16) % 4, (y + k // 4 % 4) % 4, (z + k % 4) % 4
        return ((c[1] * 4 + c[2]) * 2 + core, c[0])

    def cross_peer(k):
        return (yz * 2 + 1 - core, (x + k) % 4)

    def axis_peer(axis, k):
        c = list(xyz)
        c[axis] = (c[axis] + k) % 4
        return ((c[1] * 4 + c[2]) * 2 + core, c[0])

    def load(src, dst, n):
        return pltpu.make_async_copy(src, dst, hsem.at[n])

    own_q = qall.at[core, x, y, z]
    feat_loads = [load(feats.at[:, :, :, pl.ds(KC * k, KC)], xall[k], k) for k in range(NK)]
    wt_loads = [
        [load(wt_h.at[:, pl.ds(KC * k, KC), pl.ds(256 * h, 256)], wt.at[h, k], (4, 30)[h] + k) for k in range(NK)]
        for h in range(2)
    ]
    small = [load(a, b, 22 + n) for n, (a, b) in enumerate(zip((g1_h, s1_h, g2_h, s2_h, g3_h, s3_h), (g1, s1, g2, s2, g3, s3)))]
    small += [load(qf_h, own_q, 8), load(qf_h, qmine, 9), load(wq_h, wq, 10)]
    queue_load = load(queue_h, queue_v, 11)
    ws_load = load(ws_h, ws, 12)
    we_loads = [load(we_h.at[:, pl.ds(INNER * q, INNER)], we.at[q], 16 + q) for q in range(4)]
    wk_load = load(wk_h, wk, 14)
    feat_loads[0].start()
    wt_loads[0][0].start()
    first_loads = [load(starts_h, starts, 20), load(shuf_h, shuf, 21)]
    for d in first_loads:
        d.start()
    barrier = pltpu.get_barrier_semaphore()
    for k in range(1, CHIPS):
        pl.semaphore_signal(barrier, inc=1, device_id=chip_peer(k), device_id_type=MESH)
    for k in range(4):
        pl.semaphore_signal(barrier, inc=1, device_id=cross_peer(k), device_id_type=MESH)


    for d in first_loads:
        d.wait()
    row = shuf[...].astype(F32)
    sq = (PEERS, PEERS)
    r_i = lax.broadcasted_iota(I32, sq, 0)
    c_i = lax.broadcasted_iota(I32, sq, 1)
    wide = jnp.broadcast_to(row, sq)
    column = jnp.sum(jnp.where(r_i == c_i, wide, 0.0), axis=1, keepdims=True)
    hit = column == c_i.astype(F32)
    inverse = jnp.sum(jnp.where(hit, r_i.astype(F32), 0.0), axis=0, keepdims=True)
    tabv[x] = jnp.zeros((8, 128), I32)
    tabv[4] = jnp.zeros((8, 128), I32)
    tabv[x, 0:1, 0:PEERS] = shuf[...]
    tabv[4, 0:1, 0:PEERS] = inverse.astype(I32)

    def conv_one(k, h):
        empty = jnp.zeros((SPOTS, KC), BF16)

        def rows(p, _):
            taps = []
            for o in range(3):
                blocks = []
                for m in range(4):
                    n = p * 4 + m
                    first = starts[n] + (o - 1)
                    for t in range(FRAMES):
                        inside = 0 <= t + o - 1 < FRAMES
                        blocks.append(xall[k][n, first + t] if inside else empty)
                taps.append(jnp.concatenate(blocks, axis=0))
            lhs = jnp.concatenate(taps, axis=1)
            w = wt[h, k].reshape(3 * KC, 256)
            r = jnp.dot(lhs, w, preferred_element_type=F32)
            at = pl.ds(pl.multiple_of(p * 512, 512), 512)
            for c in range(2):
                q = 2 * h + c
                v = r[:, 128 * c : 128 * (c + 1)]
                acc[q, at, :] = v if k == 0 else acc[q, at, :] + v
            return 0

        lax.fori_loop(0, CLIPS // 4, rows, 0)

    def q_region(p, phase):
        at = [pl.ds(xyz[a], 1) for a in range(3)]
        if phase >= 1:
            at[ORDER[p][0]] = pl.ds(0, 4)
        if phase >= 2:
            at[ORDER[p][0]] = pl.ds(2 * (phase - 2), 2)
            at[ORDER[p][1]] = pl.ds(0, 4)
        return qall.at[(core, *at, slice(None), pl.ds(*PARTS[p]))]

    def q_send(phase, parts=(0, 1, 2)):
        for p in parts:
            part = q_region(p, phase)
            for k in range(1, 4):
                pltpu.make_async_remote_copy(
                    src_ref=part, dst_ref=part, send_sem=qsem.at[0, p, phase], recv_sem=qsem.at[1, p, phase],
                    device_id=axis_peer(ORDER[p][min(phase, 2)], k), device_id_type=MESH,
                ).start()

    def q_wait(phase, side, parts=(0, 1, 2)):
        for p in parts:
            cols = pl.ds(*PARTS[p])
            half_phase = qall.at[0, pl.ds(0, 3), pl.ds(0, 2), :, :, cols]
            ref = (
                qall.at[0, 0, 0, pl.ds(0, 3), :, cols],
                qall.at[0, 0, pl.ds(0, 3), :, :, cols],
                half_phase,
                half_phase,
            )[phase]
            await_bytes(ref, qsem.at[side, p, phase])

    core_copy = pltpu.make_async_remote_copy(
        src_ref=qall.at[core], dst_ref=qall.at[core], send_sem=csem.at[0], recv_sem=csem.at[1],
        device_id=(yz * 2 + 1 - core, x), device_id_type=MESH,
    )

    def plane_send(r):
        for k in range(1, PLANE):
            pltpu.make_async_remote_copy(
                src_ref=sb.at[r], dst_ref=ra[r].at[k - 1], send_sem=asem.at[0, r], recv_sem=asem.at[1, r],
                device_id=plane_peer(k), device_id_type=MESH,
            ).start()
        ra[r][PLANE - 1] = sb[r]

    def plane_forward(r):
        await_bytes(ra[r].at[pl.ds(0, PLANE - 1)], asem.at[1, r])
        for k in range(1, LINE):
            tb[r, k - 1] = ra[r][picks[0, k]] * jnp.where(picks[1, k] == 1, 1.0, 0.0).astype(F32)
            pltpu.make_async_remote_copy(
                src_ref=tb.at[r, k - 1], dst_ref=rb.at[r, k - 1], send_sem=bsem.at[0, r], recv_sem=bsem.at[1, r],
                device_id=line_peer(k), device_id_type=MESH,
            ).start()

    def line_finish(r):
        mine = ra[r][picks[0, 0]] * jnp.where(picks[1, 0] == 1, 1.0, 0.0).astype(F32)
        await_bytes(rb.at[r, pl.ds(0, LINE - 1)], bsem.at[1, r])
        for k in range(LINE - 1):
            mine = mine + rb[r, k]
        return mine

    def put_stats(r, parts, chunks=(0, 1, 2, 3)):
        if len(chunks) < 4:
            sb[r] = jnp.zeros((8, 128), F32)
        for n, q in enumerate(chunks):
            sb[r, q : q + 1, :] = jnp.sum(parts[2 * n], axis=0, keepdims=True)
            sb[r, 4 + q : 5 + q, :] = jnp.sum(parts[2 * n + 1], axis=0, keepdims=True)

    def affine(tile, gain, shift, chunks=(0, 1, 2, 3)):
        scales, shifts = [], []
        for q in chunks:
            m = tile[q : q + 1, :] * (1.0 / COUNT)
            w = tile[4 + q : 5 + q, :] * (1.0 / COUNT) - m * m
            scale = gain[:, 128 * q : 128 * (q + 1)] * lax.rsqrt(w + EPS)
            scales.append(scale)
            shifts.append(shift[:, 128 * q : 128 * (q + 1)] - m * scale)
        return jnp.concatenate(scales, axis=1), jnp.concatenate(shifts, axis=1)

    zeros = tuple(jnp.zeros((8, 128), F32) for _ in range(8))

    def sums_of(block):
        v = block.reshape(-1, 8, 128)
        return jnp.sum(v, axis=0), jnp.sum(v * v, axis=0)

    def rows_of(ref, at, chunks=(0, 1, 2, 3)):
        return jnp.concatenate([ref[q, at, :] for q in chunks], axis=1)

    def total_of(ref, chunks=(0, 1, 2, 3)):
        def body(p, carry):
            out = list(carry)
            for n, q in enumerate(chunks):
                a, b = sums_of(ref[q, pl.ds(pl.multiple_of(p * 128, 128), 128), :])
                out[2 * n] = out[2 * n] + a
                out[2 * n + 1] = out[2 * n + 1] + b
            return tuple(out)

        return lax.fori_loop(0, ROWS // 128, body, zeros[: 2 * len(chunks)])

    to_scalar = pltpu.make_async_copy(tabv, tabs, hsem.at[15])

    def find_picks():
        to_scalar.wait()
        for k in range(LINE):
            m = (member + k) % LINE
            group = tabs[m // 2, 0, yz * 2 + m % 2]
            j = tabs[4, 0, group]
            picks[0, k] = (yz - j // 2 + PLANE - 1) % PLANE
            picks[1, k] = jnp.where(j % 2 == core, 1, 0).astype(I32)

    for k in range(NK):
        feat_loads[k].wait()
        wt_loads[0][k].wait()
        for ahead in {0: (1, 2), 1: (3,)}.get(k, ()):
            feat_loads[ahead].start()
            wt_loads[0][ahead].start()
        if k == 0:
            for d in small:
                d.start()
        if k == 2:
            for d in wt_loads[1]:
                d.start()
            queue_load.start()
        if k == 3:
            ws_load.start()
            for d in we_loads:
                d.start()
            wk_load.start()
        conv_one(k, 0)
        if k == 2:
            pl.semaphore_wait(barrier, CHIPS - 1 + 4)
            for d in small:
                d.wait()
            for n in range(1, 4):
                pltpu.make_async_remote_copy(
                    src_ref=tabv.at[x], dst_ref=tabv.at[x], send_sem=tsem.at[0], recv_sem=tsem.at[1],
                    device_id=axis_peer(0, n), device_id_type=MESH,
                ).start()
            q_send(0)
    put_stats(0, total_of(acc, (0, 1)), (0, 1))
    plane_send(0)
    for k in range(NK):
        wt_loads[1][k].wait()
        conv_one(k, 1)
        if k == 1:
            q_wait(0, 1)
            q_send(1)
            await_bytes(tabv.at[pl.ds(0, 3)], tsem.at[1])
            to_scalar.start()
        if k == 2:
            find_picks()
    put_stats(6, total_of(acc, (2, 3)), (2, 3))
    plane_send(6)

    zq = jnp.dot(qmine[...], wq[...], preferred_element_type=F32)
    length = jnp.sqrt(jnp.sum(zq * zq, axis=-1, keepdims=True) + TINY)
    unit = zq / length
    unit_b = unit.astype(BF16)
    plane_forward(0)
    queue_load.wait()

    def queue_part(lo, hi, carry):
        def body(n, carry):
            total, mix = carry
            qb = queue_v[pl.ds(pl.multiple_of(n * 1024, 1024), 1024), :].astype(F32)
            inv = lax.rsqrt(jnp.sum(qb * qb, axis=-1, keepdims=True) + TINY)
            qu = (qb * inv).astype(BF16)
            neg = lax.dot_general(unit_b, qu, (((1,), (1,)), ((), ())), preferred_element_type=F32) * 5.0
            e = jnp.exp(neg)
            total = total + jnp.sum(e, axis=-1, keepdims=True)
            mix = mix + jnp.dot(e.astype(BF16), qu, preferred_element_type=F32)
            return total, mix

        return lax.fori_loop(lo, hi, body, carry)

    carry = (jnp.zeros((CLIPS, 1), F32), jnp.zeros((CLIPS, EMB), F32))
    for r in range(4):
        for e in (0, SIDE + 1):
            act[r, e] = jnp.zeros((64, INNER), BF16)

    def normalize_one(h, tile):
        chunks = (2 * h, 2 * h + 1)
        scale, shift = affine(tile, g1[...], s1[...], chunks)

        def norm_one(p, _):
            for r in range(SIDE):
                for c in range(SIDE):
                    both = [
                        rows_of(acc, pl.ds((2 * p + m) * 128 + SIDE * r + c, FRAMES, stride=SPOTS), chunks)
                        for m in range(2)
                    ]
                    v = jnp.concatenate(both, axis=0)
                    v = jnp.maximum(v * scale + shift, 0.0).astype(BF16)
                    act[r, c + 1, pl.ds(pl.multiple_of(p * 16, 16), 16), 256 * h : 256 * (h + 1)] = v
            return 0

        lax.fori_loop(0, CLIPS // 2, norm_one, 0)

    def row_conv(h, r, base, tap, taps):
        lanes = slice(256 * h, 256 * (h + 1))
        lhs = jnp.concatenate(
            [act[base + d, c : c + SIDE, :, lanes].reshape(256, 256) for d in range(taps) for c in range(3)], axis=1
        )
        w = ws[pl.ds(tap, 3 * taps), lanes].reshape(3 * taps * 256, INNER)
        v = jnp.dot(lhs, w, preferred_element_type=F32)
        at = pl.ds(pl.multiple_of(r * 256, 256), 256)
        for q in range(4):
            part = v[:, 128 * q : 128 * (q + 1)]
            second[q, at, :] = part if h == 0 else second[q, at, :] + part

    def edges(h):
        def edge(n, _):
            row_conv(h, 3 * n, 2 * n, 3 - 3 * n, 2)
            return 0

        lax.fori_loop(0, 2, edge, 0)

    def middles(h):
        def middle(n, _):
            row_conv(h, 1 + n, n, 0, 3)
            return 0

        lax.fori_loop(0, 2, middle, 0)

    carry = queue_part(0, 7, carry)
    plane_forward(6)
    q_wait(1, 1)
    q_send(2, (1, 2))
    tile = line_finish(0)
    normalize_one(0, tile)
    ws_load.wait()
    edges(0)
    middles(0)
    tile = line_finish(6)
    q_send(2, (0,))
    q_send(3, (1, 2))
    normalize_one(1, tile)
    edges(1)
    middles(1)
    put_stats(1, total_of(second))
    plane_send(1)
    q_send(3, (0,))
    carry = queue_part(7, 15, carry)
    plane_forward(1)
    carry = queue_part(15, 16, carry)
    tile = line_finish(1)
    q_wait(2, 1)
    q_wait(3, 1)
    core_copy.start()

    scale, shift = affine(tile, g2[...], s2[...])

    side = (128, 128)
    to = lax.broadcasted_iota(I32, side, 0)
    source = lax.broadcasted_iota(I32, side, 1)
    swap = jnp.where((to % 16) * 8 + to // 16 == source, 1.0, 0.0).astype(BF16)

    def norm_two(p, _):
        for n in (2 * p, 2 * p + 1):
            chunks = []
            for q in range(4):
                lanes = slice(128 * q, 128 * (q + 1))
                rows = [second[q, pl.ds(pl.multiple_of(n * 8, 8) + 64 * s, 8), :] for s in range(SPOTS)]
                v = jnp.concatenate(rows, axis=0) * scale[:, lanes] + shift[:, lanes]
                chunks.append(jnp.maximum(v, 0.0).astype(BF16))
            v = jnp.dot(swap, jnp.concatenate(chunks, axis=1), preferred_element_type=F32)
            act2[pl.ds(pl.multiple_of(n * 128, 128), 128), :] = v.astype(BF16)
        return 0

    lax.fori_loop(0, CLIPS // 2, norm_two, 0)
    for d in we_loads:
        d.wait()

    for q in range(4):
        sums = list(zeros)
        for p in range(2):
            at = pl.ds(p * 512, 512)
            v = jnp.dot(act2[at, :], we[q], preferred_element_type=F32)
            third[q, at, :] = v
            for c in range(4):
                a, b = sums_of(v[:, 128 * c : 128 * (c + 1)])
                sums[2 * c] = sums[2 * c] + a
                sums[2 * c + 1] = sums[2 * c + 1] + b
        put_stats(2 + q, sums)
        plane_send(2 + q)
    for q in range(4):
        plane_forward(2 + q)

    for q in range(4):
        cols = slice(INNER * q, INNER * (q + 1))
        scale, shift = affine(line_finish(2 + q), g3[:, cols], s3[:, cols])

        def pool(n, _):
            at = pl.ds(pl.multiple_of(n * 128, 128), 128)
            first = starts[n]
            for c in range(4):
                lanes = slice(128 * c, 128 * (c + 1))
                kept = jnp.concatenate([xall[q][n, first + t, :, lanes] for t in range(FRAMES)], axis=0).astype(F32)
                v = jnp.maximum(third[q, at, lanes] * scale[:, lanes] + shift[:, lanes] + kept, 0.0)
                pooled[n, :, INNER * q + 128 * c : INNER * q + 128 * (c + 1)] = jnp.sum(
                    v.reshape(16, 8, 128), axis=0
                )
            return 0

        lax.fori_loop(0, CLIPS, pool, 0)
    wk_load.wait()
    mean = jnp.sum(pooled[...], axis=1) * (1.0 / 128.0)
    projected = jnp.dot(mean.astype(BF16), wk[...], preferred_element_type=F32)
    norm = jnp.sum(projected * projected, axis=-1, keepdims=True) + TINY
    keys = (projected * lax.rsqrt(norm)).astype(BF16)
    keys_v[...] = keys
    keys_store = load(keys_v, keys_out, 12)
    keys_store.start()

    held = keys.astype(F32)
    total, mix = carry
    e_pos = jnp.exp(jnp.sum(unit * held, axis=-1, keepdims=True) * 5.0)
    whole = e_pos + total
    grad = (mix / whole + (e_pos / whole - 1.0) * held) * 5.0
    radial = jnp.sum(unit * grad, axis=-1, keepdims=True)
    gvec[...] = ((grad - radial * unit) / length).astype(BF16)
    for k in range(1, CHIPS):
        pltpu.make_async_remote_copy(
            src_ref=gvec, dst_ref=gall.at[chip], send_sem=gsem.at[0], recv_sem=gsem.at[1],
            device_id=chip_peer(k), device_id_type=MESH,
        ).start()
    gall[chip] = gvec[...]
    core_copy.wait_recv()

    def turn(n, _):
        cols = pl.ds(pl.multiple_of(n * 128, 128), 128)
        v = qall[:, :, :, :, :, cols].astype(F32).reshape(1024, 128)
        qt[cols, :] = v.T.astype(BF16)
        return 0

    lax.fori_loop(0, C // 128, turn, 0)
    qt_store = load(qt, qt_out, 15)
    qt_store.start()
    await_bytes(gall.at[pl.ds(0, CHIPS - 1)], gsem.at[1])
    own_half = pltpu.make_async_copy(gall, g_out.at[core], hsem.at[13])
    own_half.start()
    grads_copy = pltpu.make_async_remote_copy(
        src_ref=gall, dst_ref=g_out.at[core], send_sem=gsem.at[2], recv_sem=gsem.at[3],
        device_id=cross_peer(0), device_id_type=MESH,
    )
    grads_copy.start()
    grads_copy.wait_recv()
    own_half.wait()
    qt_store.wait()
    keys_store.wait()

    await_bytes(tabv.at[pl.ds(0, 3)], tsem.at[0])
    for phase in range(4):
        q_wait(phase, 0)
    core_copy.wait_send()
    for r in range(ROUNDS):
        await_bytes(ra[r].at[pl.ds(0, PLANE - 1)], asem.at[0, r])
        await_bytes(rb.at[r, pl.ds(0, LINE - 1)], bsem.at[0, r])
    await_bytes(gall.at[pl.ds(0, CHIPS - 1)], gsem.at[0])
    grads_copy.wait_send()


def last(keys_ref, q_ref, g_ref, keys_out, grad_out, keys_v, q_v, g_v, out_v, sem):
    tall = C // PIECES

    def rows(n):
        return pl.ds(n * tall, tall)

    keys_in = pltpu.make_async_copy(keys_ref, keys_v, sem.at[0])
    g_in = pltpu.make_async_copy(g_ref, g_v, sem.at[1])
    q_in = [pltpu.make_async_copy(q_ref.at[rows(n)], q_v.at[n], sem.at[2 + n]) for n in range(PIECES)]
    g_in.start()
    for d in q_in:
        d.start()
    keys_in.start()
    stores = []
    g_in.wait()
    for n in range(PIECES):
        q_in[n].wait()
        out_v[n] = jnp.dot(q_v[n], g_v[...], preferred_element_type=F32)
        d = pltpu.make_async_copy(out_v.at[n], grad_out.at[rows(n)], sem.at[2 + PIECES + n])
        d.start()
        stores.append(d)
    keys_in.wait()
    d = pltpu.make_async_copy(keys_v, keys_out, sem.at[0])
    d.start()
    for e in stores:
        e.wait()
    d.wait()


def local(
    key_feats, clip_starts, shuffle, query_feats, conv_time, conv_space, conv_expand,
    gain_one, shift_one, gain_two, shift_two, gain_three, shift_three, w_key, w_query, queue,
):
    hbm = pl.BlockSpec(memory_space=pltpu.HBM)
    V = pltpu.VMEM
    DMA = pltpu.SemaphoreType.DMA
    rows = [v.reshape(1, -1) for v in (gain_one, shift_one, gain_two, shift_two, gain_three, shift_three)]
    keys, q_t, grads = pl.pallas_call(
        kernel,
        name="moco",
        out_shape=(
            jax.ShapeDtypeStruct((CLIPS, EMB), BF16),
            jax.ShapeDtypeStruct((C, 1024), BF16),
            jax.ShapeDtypeStruct((2, CHIPS, CLIPS, EMB), BF16),
        ),
        in_specs=[hbm] * 16,
        out_specs=(hbm, hbm, hbm),
        scratch_shapes=[
            [V((CLIPS, TF, SPOTS, KC), BF16) for _ in range(NK)],
            V((2, NK, 3, KC, 256), BF16),
            V((4, ROWS, 128), F32),
            V((4, ROWS, 128), F32),
            V((SIDE, SIDE + 2, 64, INNER), BF16),
            V((9, INNER, INNER), BF16),
            V((ROWS, INNER), BF16),
            V((4, INNER, INNER), BF16),
            V((4, ROWS, INNER), F32),
            V((QUEUE, EMB), BF16),
            V((2, 4, 4, 4, CLIPS, C), BF16),
            V((C, 1024), BF16),
            V((C, EMB), BF16),
            V((C, EMB), BF16),
            V((5, 8, 128), I32),
            pltpu.SMEM((5, 8, 128), I32),
            pltpu.SMEM((2, LINE), I32),
            V((ROUNDS, 8, 128), F32),
            [V((PLANE, 8, 128), F32) for _ in range(ROUNDS)],
            V((ROUNDS, LINE - 1, 8, 128), F32),
            V((ROUNDS, LINE - 1, 8, 128), F32),
            V((CLIPS, C), BF16),
            V((CHIPS, CLIPS, EMB), BF16),
            V((CLIPS, 8, C), F32),
            V((CLIPS, EMB), BF16),
            V((CLIPS, EMB), BF16),
            pltpu.SMEM((CLIPS,), I32),
            V((1, PEERS), I32),
            *[V((1, n), F32) for n in (INNER,) * 4 + (C,) * 2],
            DMA((34,)),
            DMA((2, ROUNDS)),
            DMA((2, ROUNDS)),
            DMA((4,)),
            DMA((2,)),
            DMA((2, 3, 4)),
            DMA((2,)),
        ],
        compiler_params=pltpu.CompilerParams(
            collective_id=0, has_side_effects=True, vmem_limit_bytes=67043328
        ),
    )(
        clip_starts, key_feats, shuffle, query_feats, conv_time, conv_space, conv_expand,
        *rows, w_key, w_query, queue,
    )
    return pl.pallas_call(
        last,
        name="last",
        out_shape=(jax.ShapeDtypeStruct((CLIPS, EMB), BF16), jax.ShapeDtypeStruct((C, EMB), F32)),
        in_specs=[hbm] * 3,
        out_specs=(hbm, hbm),
        scratch_shapes=[
            V((CLIPS, EMB), BF16),
            V((PIECES, C // PIECES, 1024), BF16),
            V((1024, EMB), BF16),
            V((PIECES, C // PIECES, EMB), F32),
            DMA((2 + 2 * PIECES,)),
        ],
    )(keys, q_t, grads.reshape(1024, EMB))


def solution(mesh):
    placed = (
        (P(("dp", "bn"), None, None, None), P(("dp", "bn")), P("bn", None), P(("dp", "bn"), None)) + (P(),) * 12
    )
    return jax.shard_map(
        local, mesh=mesh, in_specs=placed, out_specs=(P(("dp", "bn"), None), P()), check_vma=False
    )
```

```python
import jax
import jax.numpy as jnp
from jax import lax
from jax.experimental import pallas as pl
from jax.experimental.pallas import tpu as pltpu
from jax.sharding import PartitionSpec as P

MESH = pl.DeviceIdType.MESH
F32, BF16, I32 = jnp.float32, jnp.bfloat16, jnp.int32
CLIPS, FRAMES, TF, SPOTS, SIDE, CHIPS = 8, 8, 12, 16, 4, 64
C, INNER, EMB, QUEUE = 2048, 512, 128, 16384
PLANE, LINE, PEERS, ROUNDS, PIECES = 16, 8, 32, 7, 8
KC = 512
NK = C // KC
ROWS = CLIPS * FRAMES * SPOTS
COUNT = float(4 * ROWS)
EPS, TINY = 1e-05, 1e-06
PARTS = ((0, 640), (640, 640), (1280, 768))
ORDER = ((2, 1, 0), (1, 0, 2), (0, 2, 1))


def await_bytes(ref, sem):
    pltpu.make_async_copy(ref, ref, sem).wait()


def kernel(
    starts_h, feats, shuf_h, qf_h, wt_h, ws_h, we_h, g1_h, s1_h, g2_h, s2_h, g3_h, s3_h, wk_h, wq_h, queue_h,
    keys_out, qt_out, g_out,
    xall, wt, acc, second, act, ws, act2, we, third, queue_v, qall, qt, wk, wq,
    tabv, tabs, picks, sb, ra, tb, rb, qmine, gall, pooled, gvec, keys_v,
    starts, shuf, g1, s1, g2, s2, g3, s3,
    hsem, asem, bsem, gsem, tsem, qsem, csem,
):
    i, x = lax.axis_index("dp"), lax.axis_index("bn")
    yz, core = i // 2, i % 2
    y, z = yz // 4, yz % 4
    xyz = (x, y, z)
    member = x * 2 + core
    chip = x * 16 + yz

    def plane_peer(k):
        return ((yz + k) % PLANE * 2 + core, x)

    def line_peer(k):
        m = (member + k) % LINE
        return (yz * 2 + m % 2, m // 2)

    def chip_peer(k):
        c = (x + k // 16) % 4, (y + k // 4 % 4) % 4, (z + k % 4) % 4
        return ((c[1] * 4 + c[2]) * 2 + core, c[0])

    def hops(k):
        return sum(min(d, 4 - d) for d in (k // 16, k // 4 % 4, k % 4))

    def cross_peer(k):
        return (yz * 2 + 1 - core, (x + k) % 4)

    def axis_peer(axis, k):
        c = list(xyz)
        c[axis] = (c[axis] + k) % 4
        return ((c[1] * 4 + c[2]) * 2 + core, c[0])

    def load(src, dst, n):
        return pltpu.make_async_copy(src, dst, hsem.at[n])

    own_q = qall.at[core, x, y, z]
    class Pieces:
        def __init__(self, pairs, whole, n):
            self.copies = [load(src, dst, n) for src, dst in pairs]
            self.whole, self.n = whole, n

        def start(self):
            for d in self.copies:
                d.start()

        def wait(self):
            await_bytes(self.whole, hsem.at[self.n])

    feat_loads = [
        Pieces(
            [(feats.at[pl.ds(2 * m, 2), :, :, pl.ds(KC * k, KC)], xall[k].at[pl.ds(2 * m, 2)]) for m in range(4)],
            xall[k], k,
        )
        for k in range(NK)
    ]
    wt_loads = [
        [
            Pieces(
                [(wt_h.at[o, pl.ds(KC * k, KC), pl.ds(256 * h, 256)], wt.at[h, k, o]) for o in range(3)],
                wt.at[h, k], (4, 30)[h] + k,
            )
            for k in range(NK)
        ]
        for h in range(2)
    ]
    small = [load(a, b, 22 + n) for n, (a, b) in enumerate(zip((g1_h, s1_h, g2_h, s2_h, g3_h, s3_h), (g1, s1, g2, s2, g3, s3)))]
    small += [load(qf_h, own_q, 8), load(qf_h, qmine, 9), load(wq_h, wq, 10)]
    queue_load = load(queue_h, queue_v, 11)
    ws_load = load(ws_h, ws, 12)
    we_loads = [load(we_h.at[:, pl.ds(INNER * q, INNER)], we.at[q], 16 + q) for q in range(4)]
    wk_load = load(wk_h, wk, 14)
    feat_loads[0].start()
    wt_loads[0][0].start()
    first_loads = [load(starts_h, starts, 20), load(shuf_h, shuf, 21)]
    for d in first_loads:
        d.start()
    barrier = pltpu.get_barrier_semaphore()
    for k in range(1, CHIPS):
        pl.semaphore_signal(barrier, inc=1, device_id=chip_peer(k), device_id_type=MESH)
    for k in range(4):
        pl.semaphore_signal(barrier, inc=1, device_id=cross_peer(k), device_id_type=MESH)


    for d in first_loads:
        d.wait()
    row = shuf[...].astype(F32)
    sq = (PEERS, PEERS)
    r_i = lax.broadcasted_iota(I32, sq, 0)
    c_i = lax.broadcasted_iota(I32, sq, 1)
    wide = jnp.broadcast_to(row, sq)
    column = jnp.sum(jnp.where(r_i == c_i, wide, 0.0), axis=1, keepdims=True)
    hit = column == c_i.astype(F32)
    inverse = jnp.sum(jnp.where(hit, r_i.astype(F32), 0.0), axis=0, keepdims=True)
    tabv[x] = jnp.zeros((8, 128), I32)
    tabv[4] = jnp.zeros((8, 128), I32)
    tabv[x, 0:1, 0:PEERS] = shuf[...]
    tabv[4, 0:1, 0:PEERS] = inverse.astype(I32)

    def conv_one(k, h):
        empty = jnp.zeros((SPOTS, KC), BF16)

        def rows(p, carry):
            taps = []
            for o in range(3):
                blocks = []
                for m in range(4):
                    n = p * 4 + m
                    first = starts[n] + (o - 1)
                    for t in range(FRAMES):
                        inside = 0 <= t + o - 1 < FRAMES
                        blocks.append(xall[k][n, first + t] if inside else empty)
                taps.append(jnp.concatenate(blocks, axis=0))
            lhs = jnp.concatenate(taps, axis=1)
            w = wt[h, k].reshape(3 * KC, 256)
            r = jnp.dot(lhs, w, preferred_element_type=F32)
            at = pl.ds(pl.multiple_of(p * 512, 512), 512)
            out = list(carry)
            for c in range(2):
                q = 2 * h + c
                v = r[:, 128 * c : 128 * (c + 1)]
                if k > 0:
                    v = acc[q, at, :] + v
                acc[q, at, :] = v
                if k == NK - 1:
                    a, b = sums_of(v)
                    out[2 * c] = out[2 * c] + a
                    out[2 * c + 1] = out[2 * c + 1] + b
            return tuple(out)

        return lax.fori_loop(0, CLIPS // 4, rows, zeros[:4])

    def q_region(p, phase):
        at = [pl.ds(xyz[a], 1) for a in range(3)]
        if phase >= 1:
            at[ORDER[p][0]] = pl.ds(0, 4)
        if phase >= 2:
            at[ORDER[p][0]] = pl.ds(2 * (phase - 2), 2)
            at[ORDER[p][1]] = pl.ds(0, 4)
        return qall.at[(core, *at, slice(None), pl.ds(*PARTS[p]))]

    def q_send(phase, parts=(0, 1, 2)):
        for p in parts:
            part = q_region(p, phase)
            for k in range(1, 4):
                pltpu.make_async_remote_copy(
                    src_ref=part, dst_ref=part, send_sem=qsem.at[0, p, phase], recv_sem=qsem.at[1, p, phase],
                    device_id=axis_peer(ORDER[p][min(phase, 2)], k), device_id_type=MESH,
                ).start()

    def q_wait(phase, side, parts=(0, 1, 2)):
        for p in parts:
            cols = pl.ds(*PARTS[p])
            half_phase = qall.at[0, pl.ds(0, 3), pl.ds(0, 2), :, :, cols]
            ref = (
                qall.at[0, 0, 0, pl.ds(0, 3), :, cols],
                qall.at[0, 0, pl.ds(0, 3), :, :, cols],
                half_phase,
                half_phase,
            )[phase]
            await_bytes(ref, qsem.at[side, p, phase])

    core_copy = pltpu.make_async_remote_copy(
        src_ref=qall.at[core], dst_ref=qall.at[core], send_sem=csem.at[0], recv_sem=csem.at[1],
        device_id=(yz * 2 + 1 - core, x), device_id_type=MESH,
    )

    def plane_send(r):
        for k in range(1, PLANE):
            pltpu.make_async_remote_copy(
                src_ref=sb.at[r], dst_ref=ra[r].at[k - 1], send_sem=asem.at[0, r], recv_sem=asem.at[1, r],
                device_id=plane_peer(k), device_id_type=MESH,
            ).start()
        ra[r][PLANE - 1] = sb[r]

    def plane_forward(r):
        await_bytes(ra[r].at[pl.ds(0, PLANE - 1)], asem.at[1, r])
        for k in range(1, LINE):
            tb[r, k - 1] = ra[r][picks[0, k]] * jnp.where(picks[1, k] == 1, 1.0, 0.0).astype(F32)
            pltpu.make_async_remote_copy(
                src_ref=tb.at[r, k - 1], dst_ref=rb.at[r, k - 1], send_sem=bsem.at[0, r], recv_sem=bsem.at[1, r],
                device_id=line_peer(k), device_id_type=MESH,
            ).start()

    def line_finish(r):
        mine = ra[r][picks[0, 0]] * jnp.where(picks[1, 0] == 1, 1.0, 0.0).astype(F32)
        await_bytes(rb.at[r, pl.ds(0, LINE - 1)], bsem.at[1, r])
        for k in range(LINE - 1):
            mine = mine + rb[r, k]
        return mine

    def put_stats(r, parts, chunks=(0, 1, 2, 3)):
        if len(chunks) < 4:
            sb[r] = jnp.zeros((8, 128), F32)
        for n, q in enumerate(chunks):
            sb[r, q : q + 1, :] = jnp.sum(parts[2 * n], axis=0, keepdims=True)
            sb[r, 4 + q : 5 + q, :] = jnp.sum(parts[2 * n + 1], axis=0, keepdims=True)

    def affine(tile, gain, shift, chunks=(0, 1, 2, 3)):
        scales, shifts = [], []
        for q in chunks:
            m = tile[q : q + 1, :] * (1.0 / COUNT)
            w = tile[4 + q : 5 + q, :] * (1.0 / COUNT) - m * m
            scale = gain[:, 128 * q : 128 * (q + 1)] * lax.rsqrt(w + EPS)
            scales.append(scale)
            shifts.append(shift[:, 128 * q : 128 * (q + 1)] - m * scale)
        return jnp.concatenate(scales, axis=1), jnp.concatenate(shifts, axis=1)

    zeros = tuple(jnp.zeros((8, 128), F32) for _ in range(8))

    def sums_of(block):
        v = block.reshape(-1, 8, 128)
        return jnp.sum(v, axis=0), jnp.sum(v * v, axis=0)

    def rows_of(ref, at, chunks=(0, 1, 2, 3)):
        return jnp.concatenate([ref[q, at, :] for q in chunks], axis=1)

    to_scalar = pltpu.make_async_copy(tabv, tabs, hsem.at[15])

    def find_picks():
        to_scalar.wait()
        for k in range(LINE):
            m = (member + k) % LINE
            group = tabs[m // 2, 0, yz * 2 + m % 2]
            j = tabs[4, 0, group]
            picks[0, k] = (yz - j // 2 + PLANE - 1) % PLANE
            picks[1, k] = jnp.where(j % 2 == core, 1, 0).astype(I32)

    feat_loads[1].start()
    wt_loads[0][1].start()
    for k in range(NK):
        feat_loads[k].wait()
        wt_loads[0][k].wait()
        if k == 0:
            for d in small:
                d.start()
        if k == 2:
            for d in wt_loads[1]:
                d.start()
            queue_load.start()
        if k == 3:
            ws_load.start()
            for d in we_loads:
                d.start()
            wk_load.start()
        parts = conv_one(k, 0)
        if k + 2 < NK:
            feat_loads[k + 2].start()
            wt_loads[0][k + 2].start()
        if k == 2:
            pl.semaphore_wait(barrier, CHIPS - 1 + 4)
            for d in small:
                d.wait()
            for n in range(1, 4):
                pltpu.make_async_remote_copy(
                    src_ref=tabv.at[x], dst_ref=tabv.at[x], send_sem=tsem.at[0], recv_sem=tsem.at[1],
                    device_id=axis_peer(0, n), device_id_type=MESH,
                ).start()
            q_send(0)
    put_stats(0, parts, (0, 1))
    plane_send(0)
    for k in range(NK):
        wt_loads[1][k].wait()
        parts = conv_one(k, 1)
        if k == 1:
            q_wait(0, 1)
            q_send(1)
            await_bytes(tabv.at[pl.ds(0, 3)], tsem.at[1])
            to_scalar.start()
        if k == 2:
            find_picks()
    put_stats(6, parts, (2, 3))
    plane_send(6)

    zq = jnp.dot(qmine[...], wq[...], preferred_element_type=F32)
    length = jnp.sqrt(jnp.sum(zq * zq, axis=-1, keepdims=True) + TINY)
    unit = zq / length
    unit_b = unit.astype(BF16)
    plane_forward(0)
    queue_load.wait()

    def queue_part(lo, hi, carry):
        def body(n, carry):
            total, mix = carry
            qb = queue_v[pl.ds(pl.multiple_of(n * 1024, 1024), 1024), :].astype(F32)
            inv = lax.rsqrt(jnp.sum(qb * qb, axis=-1, keepdims=True) + TINY)
            qu = (qb * inv).astype(BF16)
            neg = lax.dot_general(unit_b, qu, (((1,), (1,)), ((), ())), preferred_element_type=F32) * 5.0
            e = jnp.exp(neg)
            total = total + jnp.sum(e, axis=-1, keepdims=True)
            mix = mix + jnp.dot(e.astype(BF16), qu, preferred_element_type=F32)
            return total, mix

        return lax.fori_loop(lo, hi, body, carry)

    carry = (jnp.zeros((CLIPS, 1), F32), jnp.zeros((CLIPS, EMB), F32))
    for r in range(4):
        for e in (0, SIDE + 1):
            act[r, e] = jnp.zeros((64, INNER), BF16)

    def normalize_one(h, tile):
        chunks = (2 * h, 2 * h + 1)
        scale, shift = affine(tile, g1[...], s1[...], chunks)

        def norm_one(p, _):
            for r in range(SIDE):
                for c in range(SIDE):
                    both = [
                        rows_of(acc, pl.ds((2 * p + m) * 128 + SIDE * r + c, FRAMES, stride=SPOTS), chunks)
                        for m in range(2)
                    ]
                    v = jnp.concatenate(both, axis=0)
                    v = jnp.maximum(v * scale + shift, 0.0).astype(BF16)
                    act[r, c + 1, pl.ds(pl.multiple_of(p * 16, 16), 16), 256 * h : 256 * (h + 1)] = v
            return 0

        lax.fori_loop(0, CLIPS // 2, norm_one, 0)

    def row_conv(h, r, base, tap, taps, carry):
        lanes = slice(256 * h, 256 * (h + 1))
        lhs = jnp.concatenate(
            [act[base + d, c : c + SIDE, :, lanes].reshape(256, 256) for d in range(taps) for c in range(3)], axis=1
        )
        w = ws[pl.ds(tap, 3 * taps), lanes].reshape(3 * taps * 256, INNER)
        v = jnp.dot(lhs, w, preferred_element_type=F32)
        at = pl.ds(pl.multiple_of(r * 256, 256), 256)
        out = list(carry)
        for q in range(4):
            part = v[:, 128 * q : 128 * (q + 1)]
            if h == 1:
                part = second[q, at, :] + part
                a, b = sums_of(part)
                out[2 * q] = out[2 * q] + a
                out[2 * q + 1] = out[2 * q + 1] + b
            second[q, at, :] = part
        return tuple(out)

    def edges(h, sums):
        def edge(n, sums):
            return row_conv(h, 3 * n, 2 * n, 3 - 3 * n, 2, sums)

        return lax.fori_loop(0, 2, edge, sums)

    def middles(h, sums):
        def middle(n, sums):
            return row_conv(h, 1 + n, n, 0, 3, sums)

        return lax.fori_loop(0, 2, middle, sums)

    carry = queue_part(0, 5, carry)
    plane_forward(6)
    q_wait(1, 1)
    q_send(2, (1, 2))
    tile = line_finish(0)
    normalize_one(0, tile)
    ws_load.wait()
    edges(0, ())
    middles(0, ())
    tile = line_finish(6)
    q_send(2, (0,))
    q_send(3, (1, 2))
    normalize_one(1, tile)
    sums = middles(1, edges(1, zeros))
    put_stats(1, sums)
    plane_send(1)
    q_send(3, (0,))
    carry = queue_part(5, 13, carry)
    plane_forward(1)
    carry = queue_part(13, 16, carry)
    tile = line_finish(1)
    q_wait(2, 1)
    q_wait(3, 1)
    core_copy.start()

    scale, shift = affine(tile, g2[...], s2[...])

    side = (128, 128)
    to = lax.broadcasted_iota(I32, side, 0)
    source = lax.broadcasted_iota(I32, side, 1)
    swap = jnp.where((to % 16) * 8 + to // 16 == source, 1.0, 0.0).astype(BF16)

    def norm_two(p, _):
        for n in (2 * p, 2 * p + 1):
            chunks = []
            for q in range(4):
                lanes = slice(128 * q, 128 * (q + 1))
                rows = [second[q, pl.ds(pl.multiple_of(n * 8, 8) + 64 * s, 8), :] for s in range(SPOTS)]
                v = jnp.concatenate(rows, axis=0) * scale[:, lanes] + shift[:, lanes]
                chunks.append(jnp.maximum(v, 0.0).astype(BF16))
            v = jnp.dot(swap, jnp.concatenate(chunks, axis=1), preferred_element_type=F32)
            act2[pl.ds(pl.multiple_of(n * 128, 128), 128), :] = v.astype(BF16)
        return 0

    lax.fori_loop(0, CLIPS // 2, norm_two, 0)
    for d in we_loads:
        d.wait()

    for q in range(4):
        sums = list(zeros)
        for p in range(2):
            at = pl.ds(p * 512, 512)
            v = jnp.dot(act2[at, :], we[q], preferred_element_type=F32)
            third[q, at, :] = v
            for c in range(4):
                a, b = sums_of(v[:, 128 * c : 128 * (c + 1)])
                sums[2 * c] = sums[2 * c] + a
                sums[2 * c + 1] = sums[2 * c + 1] + b
        put_stats(2 + q, sums)
        plane_send(2 + q)
    for q in range(4):
        plane_forward(2 + q)

    for q in range(4):
        cols = slice(INNER * q, INNER * (q + 1))
        scale, shift = affine(line_finish(2 + q), g3[:, cols], s3[:, cols])

        def pool(n, _):
            at = pl.ds(pl.multiple_of(n * 128, 128), 128)
            first = starts[n]
            for c in range(4):
                lanes = slice(128 * c, 128 * (c + 1))
                kept = jnp.concatenate([xall[q][n, first + t, :, lanes] for t in range(FRAMES)], axis=0).astype(F32)
                v = jnp.maximum(third[q, at, lanes] * scale[:, lanes] + shift[:, lanes] + kept, 0.0)
                pooled[n, :, INNER * q + 128 * c : INNER * q + 128 * (c + 1)] = jnp.sum(
                    v.reshape(16, 8, 128), axis=0
                )
            return 0

        lax.fori_loop(0, CLIPS, pool, 0)
    wk_load.wait()
    mean = jnp.sum(pooled[...], axis=1) * (1.0 / 128.0)
    projected = jnp.dot(mean.astype(BF16), wk[...], preferred_element_type=F32)
    norm = jnp.sum(projected * projected, axis=-1, keepdims=True) + TINY
    keys = (projected * lax.rsqrt(norm)).astype(BF16)
    keys_v[...] = keys
    keys_store = load(keys_v, keys_out, 12)
    keys_store.start()

    held = keys.astype(F32)
    total, mix = carry
    e_pos = jnp.exp(jnp.sum(unit * held, axis=-1, keepdims=True) * 5.0)
    whole = e_pos + total
    grad = (mix / whole + (e_pos / whole - 1.0) * held) * 5.0
    radial = jnp.sum(unit * grad, axis=-1, keepdims=True)
    gvec[...] = ((grad - radial * unit) / length).astype(BF16)
    for k in sorted(range(1, CHIPS), key=hops, reverse=True):
        pltpu.make_async_remote_copy(
            src_ref=gvec, dst_ref=gall.at[chip], send_sem=gsem.at[0], recv_sem=gsem.at[1],
            device_id=chip_peer(k), device_id_type=MESH,
        ).start()
    gall[chip] = gvec[...]
    core_copy.wait_recv()

    def turn(n, _):
        cols = pl.ds(pl.multiple_of(n * 128, 128), 128)
        v = qall[:, :, :, :, :, cols].astype(F32).reshape(1024, 128)
        qt[cols, :] = v.T.astype(BF16)
        return 0

    lax.fori_loop(0, C // 128, turn, 0)
    qt_store = load(qt, qt_out, 15)
    qt_store.start()
    await_bytes(gall.at[pl.ds(0, CHIPS - 1)], gsem.at[1])
    own_half = pltpu.make_async_copy(gall, g_out.at[core], hsem.at[13])
    own_half.start()
    grads_copy = pltpu.make_async_remote_copy(
        src_ref=gall, dst_ref=g_out.at[core], send_sem=gsem.at[2], recv_sem=gsem.at[3],
        device_id=cross_peer(0), device_id_type=MESH,
    )
    grads_copy.start()
    grads_copy.wait_recv()
    own_half.wait()
    qt_store.wait()
    keys_store.wait()

    await_bytes(tabv.at[pl.ds(0, 3)], tsem.at[0])
    for phase in range(4):
        q_wait(phase, 0)
    core_copy.wait_send()
    for r in range(ROUNDS):
        await_bytes(ra[r].at[pl.ds(0, PLANE - 1)], asem.at[0, r])
        await_bytes(rb.at[r, pl.ds(0, LINE - 1)], bsem.at[0, r])
    await_bytes(gall.at[pl.ds(0, CHIPS - 1)], gsem.at[0])
    grads_copy.wait_send()


def last(keys_ref, q_ref, g_ref, keys_out, grad_out, keys_v, q_v, g_v, out_v, sem):
    tall = C // PIECES

    def rows(n):
        return pl.ds(n * tall, tall)

    keys_in = pltpu.make_async_copy(keys_ref, keys_v, sem.at[0])
    g_in = pltpu.make_async_copy(g_ref, g_v, sem.at[1])
    q_in = [pltpu.make_async_copy(q_ref.at[rows(n)], q_v.at[n], sem.at[2 + n]) for n in range(PIECES)]
    g_in.start()
    for d in q_in:
        d.start()
    keys_in.start()
    stores = []
    g_in.wait()
    for n in range(PIECES):
        q_in[n].wait()
        out_v[n] = jnp.dot(q_v[n], g_v[...], preferred_element_type=F32)
        d = pltpu.make_async_copy(out_v.at[n], grad_out.at[rows(n)], sem.at[2 + PIECES + n])
        d.start()
        stores.append(d)
    keys_in.wait()
    d = pltpu.make_async_copy(keys_v, keys_out, sem.at[0])
    d.start()
    for e in stores:
        e.wait()
    d.wait()


def local(
    key_feats, clip_starts, shuffle, query_feats, conv_time, conv_space, conv_expand,
    gain_one, shift_one, gain_two, shift_two, gain_three, shift_three, w_key, w_query, queue,
):
    hbm = pl.BlockSpec(memory_space=pltpu.HBM)
    V = pltpu.VMEM
    DMA = pltpu.SemaphoreType.DMA
    rows = [v.reshape(1, -1) for v in (gain_one, shift_one, gain_two, shift_two, gain_three, shift_three)]
    keys, q_t, grads = pl.pallas_call(
        kernel,
        name="moco",
        out_shape=(
            jax.ShapeDtypeStruct((CLIPS, EMB), BF16),
            jax.ShapeDtypeStruct((C, 1024), BF16),
            jax.ShapeDtypeStruct((2, CHIPS, CLIPS, EMB), BF16),
        ),
        in_specs=[hbm] * 16,
        out_specs=(hbm, hbm, hbm),
        scratch_shapes=[
            [V((CLIPS, TF, SPOTS, KC), BF16) for _ in range(NK)],
            V((2, NK, 3, KC, 256), BF16),
            V((4, ROWS, 128), F32),
            V((4, ROWS, 128), F32),
            V((SIDE, SIDE + 2, 64, INNER), BF16),
            V((9, INNER, INNER), BF16),
            V((ROWS, INNER), BF16),
            V((4, INNER, INNER), BF16),
            V((4, ROWS, INNER), F32),
            V((QUEUE, EMB), BF16),
            V((2, 4, 4, 4, CLIPS, C), BF16),
            V((C, 1024), BF16),
            V((C, EMB), BF16),
            V((C, EMB), BF16),
            V((5, 8, 128), I32),
            pltpu.SMEM((5, 8, 128), I32),
            pltpu.SMEM((2, LINE), I32),
            V((ROUNDS, 8, 128), F32),
            [V((PLANE, 8, 128), F32) for _ in range(ROUNDS)],
            V((ROUNDS, LINE - 1, 8, 128), F32),
            V((ROUNDS, LINE - 1, 8, 128), F32),
            V((CLIPS, C), BF16),
            V((CHIPS, CLIPS, EMB), BF16),
            V((CLIPS, 8, C), F32),
            V((CLIPS, EMB), BF16),
            V((CLIPS, EMB), BF16),
            pltpu.SMEM((CLIPS,), I32),
            V((1, PEERS), I32),
            *[V((1, n), F32) for n in (INNER,) * 4 + (C,) * 2],
            DMA((34,)),
            DMA((2, ROUNDS)),
            DMA((2, ROUNDS)),
            DMA((4,)),
            DMA((2,)),
            DMA((2, 3, 4)),
            DMA((2,)),
        ],
        compiler_params=pltpu.CompilerParams(
            collective_id=0, has_side_effects=True, vmem_limit_bytes=67043328
        ),
    )(
        clip_starts, key_feats, shuffle, query_feats, conv_time, conv_space, conv_expand,
        *rows, w_key, w_query, queue,
    )
    return pl.pallas_call(
        last,
        name="last",
        out_shape=(jax.ShapeDtypeStruct((CLIPS, EMB), BF16), jax.ShapeDtypeStruct((C, EMB), F32)),
        in_specs=[hbm] * 3,
        out_specs=(hbm, hbm),
        scratch_shapes=[
            V((CLIPS, EMB), BF16),
            V((PIECES, C // PIECES, 1024), BF16),
            V((1024, EMB), BF16),
            V((PIECES, C // PIECES, EMB), F32),
            DMA((2 + 2 * PIECES,)),
        ],
    )(keys, q_t, grads.reshape(1024, EMB))


def solution(mesh):
    placed = (
        (P(("dp", "bn"), None, None, None), P(("dp", "bn")), P("bn", None), P(("dp", "bn"), None)) + (P(),) * 12
    )
    return jax.shard_map(
        local, mesh=mesh, in_specs=placed, out_specs=(P(("dp", "bn"), None), P()), check_vma=False
    )
```

```python
import jax
import jax.numpy as jnp
from jax import lax
from jax.experimental import pallas as pl
from jax.experimental.pallas import tpu as pltpu
from jax.sharding import PartitionSpec as P

MESH = pl.DeviceIdType.MESH
F32, BF16, I32 = jnp.float32, jnp.bfloat16, jnp.int32
CLIPS, FRAMES, TF, SPOTS, SIDE, CHIPS = 8, 8, 12, 16, 4, 64
C, INNER, EMB, QUEUE = 2048, 512, 128, 16384
PLANE, LINE, PEERS, ROUNDS, PIECES = 16, 8, 32, 7, 8
KC = 512
NK = C // KC
ROWS = CLIPS * FRAMES * SPOTS
COUNT = float(4 * ROWS)
EPS, TINY = 1e-05, 1e-06
PARTS = ((0, 640), (640, 640), (1280, 768))
ORDER = ((2, 1, 0), (1, 0, 2), (0, 2, 1))


def await_bytes(ref, sem):
    pltpu.make_async_copy(ref, ref, sem).wait()


def kernel(
    starts_h, feats, shuf_h, qf_h, wt_h, ws_h, we_h, g1_h, s1_h, g2_h, s2_h, g3_h, s3_h, wk_h, wq_h, queue_h,
    keys_out, qt_out, g_out,
    xall, wt, acc, second, act, ws, act2, we, third, queue_v, qall, qt, wk, wq,
    tabv, tabs, picks, sb, ra, tb, rb, qmine, gall, pooled, gvec, keys_v,
    starts, shuf, g1, s1, g2, s2, g3, s3,
    hsem, asem, bsem, gsem, tsem, qsem, csem,
):
    i, x = lax.axis_index("dp"), lax.axis_index("bn")
    yz, core = i // 2, i % 2
    y, z = yz // 4, yz % 4
    xyz = (x, y, z)
    member = x * 2 + core
    chip = x * 16 + yz

    def plane_peer(k):
        return ((yz + k) % PLANE * 2 + core, x)

    def line_peer(k):
        m = (member + k) % LINE
        return (yz * 2 + m % 2, m // 2)

    def chip_peer(k):
        c = (x + k // 16) % 4, (y + k // 4 % 4) % 4, (z + k % 4) % 4
        return ((c[1] * 4 + c[2]) * 2 + core, c[0])

    def hops(k):
        return sum(min(d, 4 - d) for d in (k // 16, k // 4 % 4, k % 4))

    def cross_peer(k):
        return (yz * 2 + 1 - core, (x + k) % 4)

    def axis_peer(axis, k):
        c = list(xyz)
        c[axis] = (c[axis] + k) % 4
        return ((c[1] * 4 + c[2]) * 2 + core, c[0])

    def load(src, dst, n):
        return pltpu.make_async_copy(src, dst, hsem.at[n])

    own_q = qall.at[core, x, y, z]
    class Pieces:
        def __init__(self, pairs, whole, n):
            self.copies = [load(src, dst, n) for src, dst in pairs]
            self.whole, self.n = whole, n

        def start(self):
            for d in self.copies:
                d.start()

        def wait(self):
            await_bytes(self.whole, hsem.at[self.n])

    feat_loads = [
        Pieces(
            [(feats.at[pl.ds(2 * m, 2), :, :, pl.ds(KC * k, KC)], xall[k].at[pl.ds(2 * m, 2)]) for m in range(4)],
            xall[k], k,
        )
        for k in range(NK)
    ]
    wt_loads = [
        [
            Pieces(
                [(wt_h.at[o, pl.ds(KC * k, KC), pl.ds(256 * h, 256)], wt.at[h, k, o]) for o in range(3)],
                wt.at[h, k], (4, 30)[h] + k,
            )
            for k in range(NK)
        ]
        for h in range(2)
    ]
    small = [load(a, b, 22 + n) for n, (a, b) in enumerate(zip((g1_h, s1_h, g2_h, s2_h, g3_h, s3_h), (g1, s1, g2, s2, g3, s3)))]
    small += [load(qf_h, own_q, 8), load(qf_h, qmine, 9), load(wq_h, wq, 10)]
    queue_load = load(queue_h, queue_v, 11)
    ws_load = load(ws_h, ws, 12)
    we_loads = [load(we_h.at[:, pl.ds(INNER * q, INNER)], we.at[q], 16 + q) for q in range(4)]
    wk_load = load(wk_h, wk, 14)
    feat_loads[0].start()
    wt_loads[0][0].start()
    first_loads = [load(starts_h, starts, 20), load(shuf_h, shuf, 21)]
    for d in first_loads:
        d.start()
    barrier = pltpu.get_barrier_semaphore()
    for k in range(1, CHIPS):
        pl.semaphore_signal(barrier, inc=1, device_id=chip_peer(k), device_id_type=MESH)
    for k in range(4):
        pl.semaphore_signal(barrier, inc=1, device_id=cross_peer(k), device_id_type=MESH)


    for d in first_loads:
        d.wait()
    row = shuf[...].astype(F32)
    sq = (PEERS, PEERS)
    r_i = lax.broadcasted_iota(I32, sq, 0)
    c_i = lax.broadcasted_iota(I32, sq, 1)
    wide = jnp.broadcast_to(row, sq)
    column = jnp.sum(jnp.where(r_i == c_i, wide, 0.0), axis=1, keepdims=True)
    hit = column == c_i.astype(F32)
    inverse = jnp.sum(jnp.where(hit, r_i.astype(F32), 0.0), axis=0, keepdims=True)
    tabv[x] = jnp.zeros((8, 128), I32)
    tabv[4] = jnp.zeros((8, 128), I32)
    tabv[x, 0:1, 0:PEERS] = shuf[...]
    tabv[4, 0:1, 0:PEERS] = inverse.astype(I32)

    def conv_one(k, h):
        empty = jnp.zeros((SPOTS, KC), BF16)

        def rows(p, carry):
            taps = []
            for o in range(3):
                blocks = []
                for m in range(4):
                    n = p * 4 + m
                    first = starts[n] + (o - 1)
                    for t in range(FRAMES):
                        inside = 0 <= t + o - 1 < FRAMES
                        blocks.append(xall[k][n, first + t] if inside else empty)
                taps.append(jnp.concatenate(blocks, axis=0))
            lhs = jnp.concatenate(taps, axis=1)
            w = wt[h, k].reshape(3 * KC, 256)
            r = jnp.dot(lhs, w, preferred_element_type=F32)
            at = pl.ds(p * 512, 512)
            out = list(carry)
            for c in range(2):
                q = 2 * h + c
                v = r[:, 128 * c : 128 * (c + 1)]
                if k > 0:
                    v = acc[q, at, :] + v
                acc[q, at, :] = v
                if k == NK - 1:
                    a, b = sums_of(v)
                    out[2 * c] = out[2 * c] + a
                    out[2 * c + 1] = out[2 * c + 1] + b
            return tuple(out)

        return rows(1, rows(0, zeros[:4]))

    def q_region(p, phase):
        at = [pl.ds(xyz[a], 1) for a in range(3)]
        if phase >= 1:
            at[ORDER[p][0]] = pl.ds(0, 4)
        if phase >= 2:
            at[ORDER[p][0]] = pl.ds(2 * (phase - 2), 2)
            at[ORDER[p][1]] = pl.ds(0, 4)
        return qall.at[(core, *at, slice(None), pl.ds(*PARTS[p]))]

    def q_send(phase, parts=(0, 1, 2)):
        for p in parts:
            part = q_region(p, phase)
            for k in range(1, 4):
                pltpu.make_async_remote_copy(
                    src_ref=part, dst_ref=part, send_sem=qsem.at[0, p, phase], recv_sem=qsem.at[1, p, phase],
                    device_id=axis_peer(ORDER[p][min(phase, 2)], k), device_id_type=MESH,
                ).start()

    def q_wait(phase, side, parts=(0, 1, 2)):
        for p in parts:
            cols = pl.ds(*PARTS[p])
            half_phase = qall.at[0, pl.ds(0, 3), pl.ds(0, 2), :, :, cols]
            ref = (
                qall.at[0, 0, 0, pl.ds(0, 3), :, cols],
                qall.at[0, 0, pl.ds(0, 3), :, :, cols],
                half_phase,
                half_phase,
            )[phase]
            await_bytes(ref, qsem.at[side, p, phase])

    core_copy = pltpu.make_async_remote_copy(
        src_ref=qall.at[core], dst_ref=qall.at[core], send_sem=csem.at[0], recv_sem=csem.at[1],
        device_id=(yz * 2 + 1 - core, x), device_id_type=MESH,
    )

    def plane_send(r):
        for k in range(1, PLANE):
            pltpu.make_async_remote_copy(
                src_ref=sb.at[r], dst_ref=ra[r].at[k - 1], send_sem=asem.at[0, r], recv_sem=asem.at[1, r],
                device_id=plane_peer(k), device_id_type=MESH,
            ).start()
        ra[r][PLANE - 1] = sb[r]

    def plane_forward(r):
        await_bytes(ra[r].at[pl.ds(0, PLANE - 1)], asem.at[1, r])
        for k in range(1, LINE):
            tb[r, k - 1] = ra[r][picks[0, k]] * jnp.where(picks[1, k] == 1, 1.0, 0.0).astype(F32)
            pltpu.make_async_remote_copy(
                src_ref=tb.at[r, k - 1], dst_ref=rb.at[r, k - 1], send_sem=bsem.at[0, r], recv_sem=bsem.at[1, r],
                device_id=line_peer(k), device_id_type=MESH,
            ).start()

    def line_finish(r):
        mine = ra[r][picks[0, 0]] * jnp.where(picks[1, 0] == 1, 1.0, 0.0).astype(F32)
        await_bytes(rb.at[r, pl.ds(0, LINE - 1)], bsem.at[1, r])
        for k in range(LINE - 1):
            mine = mine + rb[r, k]
        return mine

    def put_stats(r, parts, chunks=(0, 1, 2, 3)):
        if len(chunks) < 4:
            sb[r] = jnp.zeros((8, 128), F32)
        for n, q in enumerate(chunks):
            sb[r, q : q + 1, :] = jnp.sum(parts[2 * n], axis=0, keepdims=True)
            sb[r, 4 + q : 5 + q, :] = jnp.sum(parts[2 * n + 1], axis=0, keepdims=True)

    def affine(tile, gain, shift, chunks=(0, 1, 2, 3)):
        scales, shifts = [], []
        for q in chunks:
            m = tile[q : q + 1, :] * (1.0 / COUNT)
            w = tile[4 + q : 5 + q, :] * (1.0 / COUNT) - m * m
            scale = gain[:, 128 * q : 128 * (q + 1)] * lax.rsqrt(w + EPS)
            scales.append(scale)
            shifts.append(shift[:, 128 * q : 128 * (q + 1)] - m * scale)
        return jnp.concatenate(scales, axis=1), jnp.concatenate(shifts, axis=1)

    zeros = tuple(jnp.zeros((8, 128), F32) for _ in range(8))

    def sums_of(block):
        v = block.reshape(-1, 8, 128)
        return jnp.sum(v, axis=0), jnp.sum(v * v, axis=0)

    def rows_of(ref, at, chunks=(0, 1, 2, 3)):
        return jnp.concatenate([ref[q, at, :] for q in chunks], axis=1)

    to_scalar = pltpu.make_async_copy(tabv, tabs, hsem.at[15])

    def find_picks():
        to_scalar.wait()
        for k in range(LINE):
            m = (member + k) % LINE
            group = tabs[m // 2, 0, yz * 2 + m % 2]
            j = tabs[4, 0, group]
            picks[0, k] = (yz - j // 2 + PLANE - 1) % PLANE
            picks[1, k] = jnp.where(j % 2 == core, 1, 0).astype(I32)

    feat_loads[1].start()
    wt_loads[0][1].start()
    for k in range(NK):
        feat_loads[k].wait()
        wt_loads[0][k].wait()
        if k == 0:
            for d in small:
                d.start()
        if k == 2:
            for d in wt_loads[1]:
                d.start()
            queue_load.start()
        if k == 3:
            ws_load.start()
            for d in we_loads:
                d.start()
            wk_load.start()
        parts = conv_one(k, 0)
        if k + 2 < NK:
            feat_loads[k + 2].start()
            wt_loads[0][k + 2].start()
        if k == 2:
            pl.semaphore_wait(barrier, CHIPS - 1 + 4)
            for d in small:
                d.wait()
            for n in range(1, 4):
                pltpu.make_async_remote_copy(
                    src_ref=tabv.at[x], dst_ref=tabv.at[x], send_sem=tsem.at[0], recv_sem=tsem.at[1],
                    device_id=axis_peer(0, n), device_id_type=MESH,
                ).start()
            q_send(0)
    put_stats(0, parts, (0, 1))
    plane_send(0)
    for k in range(NK):
        wt_loads[1][k].wait()
        parts = conv_one(k, 1)
        if k == 2:
            q_wait(0, 1)
            q_send(1)
            await_bytes(tabv.at[pl.ds(0, 3)], tsem.at[1])
            to_scalar.start()
        if k == 3:
            find_picks()
    put_stats(6, parts, (2, 3))
    plane_send(6)

    zq = jnp.dot(qmine[...], wq[...], preferred_element_type=F32)
    length = jnp.sqrt(jnp.sum(zq * zq, axis=-1, keepdims=True) + TINY)
    unit = zq / length
    unit_b = unit.astype(BF16)
    plane_forward(0)
    queue_load.wait()

    def queue_part(lo, hi, carry):
        def body(n, carry):
            total, mix = carry
            qb = queue_v[pl.ds(pl.multiple_of(n * 1024, 1024), 1024), :].astype(F32)
            inv = lax.rsqrt(jnp.sum(qb * qb, axis=-1, keepdims=True) + TINY)
            qu = (qb * inv).astype(BF16)
            neg = lax.dot_general(unit_b, qu, (((1,), (1,)), ((), ())), preferred_element_type=F32) * 5.0
            e = jnp.exp(neg)
            total = total + jnp.sum(e, axis=-1, keepdims=True)
            mix = mix + jnp.dot(e.astype(BF16), qu, preferred_element_type=F32)
            return total, mix

        return lax.fori_loop(lo, hi, body, carry)

    carry = (jnp.zeros((CLIPS, 1), F32), jnp.zeros((CLIPS, EMB), F32))
    for r in range(4):
        for e in (0, SIDE + 1):
            act[r, e] = jnp.zeros((64, INNER), BF16)

    def normalize_one(h, tile):
        chunks = (2 * h, 2 * h + 1)
        scale, shift = affine(tile, g1[...], s1[...], chunks)

        def norm_one(p, _):
            for r in range(SIDE):
                for c in range(SIDE):
                    both = [
                        rows_of(acc, pl.ds((2 * p + m) * 128 + SIDE * r + c, FRAMES, stride=SPOTS), chunks)
                        for m in range(2)
                    ]
                    v = jnp.concatenate(both, axis=0)
                    v = jnp.maximum(v * scale + shift, 0.0).astype(BF16)
                    act[r, c + 1, pl.ds(pl.multiple_of(p * 16, 16), 16), 256 * h : 256 * (h + 1)] = v
            return 0

        lax.fori_loop(0, CLIPS // 2, norm_one, 0)

    def row_conv(h, r, base, tap, taps, carry):
        lanes = slice(256 * h, 256 * (h + 1))
        lhs = jnp.concatenate(
            [act[base + d, c : c + SIDE, :, lanes].reshape(256, 256) for d in range(taps) for c in range(3)], axis=1
        )
        w = ws[pl.ds(tap, 3 * taps), lanes].reshape(3 * taps * 256, INNER)
        v = jnp.dot(lhs, w, preferred_element_type=F32)
        at = pl.ds(r * 256, 256)
        out = list(carry)
        for q in range(4):
            part = v[:, 128 * q : 128 * (q + 1)]
            if h == 1:
                part = second[q, at, :] + part
                a, b = sums_of(part)
                out[2 * q] = out[2 * q] + a
                out[2 * q + 1] = out[2 * q + 1] + b
            second[q, at, :] = part
        return tuple(out)

    def edges(h, sums):
        def edge(n, sums):
            return row_conv(h, 3 * n, 2 * n, 3 - 3 * n, 2, sums)

        return edge(1, edge(0, sums))

    def middles(h, sums):
        def middle(n, sums):
            return row_conv(h, 1 + n, n, 0, 3, sums)

        return middle(1, middle(0, sums))

    carry = queue_part(0, 5, carry)
    plane_forward(6)
    q_wait(1, 1)
    q_send(2, (1, 2))
    tile = line_finish(0)
    normalize_one(0, tile)
    ws_load.wait()
    edges(0, ())
    middles(0, ())
    tile = line_finish(6)
    q_send(2, (0,))
    q_send(3, (1, 2))
    normalize_one(1, tile)
    sums = middles(1, edges(1, zeros))
    put_stats(1, sums)
    plane_send(1)
    q_send(3, (0,))
    carry = queue_part(5, 13, carry)
    plane_forward(1)
    carry = queue_part(13, 16, carry)
    tile = line_finish(1)
    q_wait(2, 1)
    q_wait(3, 1)
    core_copy.start()

    scale, shift = affine(tile, g2[...], s2[...])

    side = (128, 128)
    to = lax.broadcasted_iota(I32, side, 0)
    source = lax.broadcasted_iota(I32, side, 1)
    swap = jnp.where((to % 16) * 8 + to // 16 == source, 1.0, 0.0).astype(BF16)

    def norm_two(p, _):
        for n in (2 * p, 2 * p + 1):
            chunks = []
            for q in range(4):
                lanes = slice(128 * q, 128 * (q + 1))
                rows = [second[q, pl.ds(pl.multiple_of(n * 8, 8) + 64 * s, 8), :] for s in range(SPOTS)]
                v = jnp.concatenate(rows, axis=0) * scale[:, lanes] + shift[:, lanes]
                chunks.append(jnp.maximum(v, 0.0).astype(BF16))
            v = jnp.dot(swap, jnp.concatenate(chunks, axis=1), preferred_element_type=F32)
            act2[pl.ds(pl.multiple_of(n * 128, 128), 128), :] = v.astype(BF16)
        return 0

    lax.fori_loop(0, CLIPS // 2, norm_two, 0)
    for d in we_loads:
        d.wait()

    for q in range(4):
        sums = list(zeros)
        for p in range(2):
            at = pl.ds(p * 512, 512)
            v = jnp.dot(act2[at, :], we[q], preferred_element_type=F32)
            third[q, at, :] = v
            for c in range(4):
                a, b = sums_of(v[:, 128 * c : 128 * (c + 1)])
                sums[2 * c] = sums[2 * c] + a
                sums[2 * c + 1] = sums[2 * c + 1] + b
        put_stats(2 + q, sums)
        plane_send(2 + q)
    for q in range(4):
        plane_forward(2 + q)

    for q in range(4):
        cols = slice(INNER * q, INNER * (q + 1))
        scale, shift = affine(line_finish(2 + q), g3[:, cols], s3[:, cols])

        def pool(pair, _):
            for n in (2 * pair, 2 * pair + 1):
                at = pl.ds(pl.multiple_of(n * 128, 128), 128)
                first = starts[n]
                for c in range(4):
                    lanes = slice(128 * c, 128 * (c + 1))
                    kept = jnp.concatenate([xall[q][n, first + t, :, lanes] for t in range(FRAMES)], axis=0).astype(F32)
                    v = jnp.maximum(third[q, at, lanes] * scale[:, lanes] + shift[:, lanes] + kept, 0.0)
                    pooled[n, :, INNER * q + 128 * c : INNER * q + 128 * (c + 1)] = jnp.sum(
                        v.reshape(16, 8, 128), axis=0
                    )
            return 0

        lax.fori_loop(0, CLIPS // 2, pool, 0)
    wk_load.wait()
    mean = jnp.sum(pooled[...], axis=1) * (1.0 / 128.0)
    projected = jnp.dot(mean.astype(BF16), wk[...], preferred_element_type=F32)
    norm = jnp.sum(projected * projected, axis=-1, keepdims=True) + TINY
    keys = (projected * lax.rsqrt(norm)).astype(BF16)
    keys_v[...] = keys
    keys_store = load(keys_v, keys_out, 12)
    keys_store.start()

    held = keys.astype(F32)
    total, mix = carry
    e_pos = jnp.exp(jnp.sum(unit * held, axis=-1, keepdims=True) * 5.0)
    whole = e_pos + total
    grad = (mix / whole + (e_pos / whole - 1.0) * held) * 5.0
    radial = jnp.sum(unit * grad, axis=-1, keepdims=True)
    gvec[...] = ((grad - radial * unit) / length).astype(BF16)
    for k in sorted(range(1, CHIPS), key=hops, reverse=True):
        pltpu.make_async_remote_copy(
            src_ref=gvec, dst_ref=gall.at[chip], send_sem=gsem.at[0], recv_sem=gsem.at[1],
            device_id=chip_peer(k), device_id_type=MESH,
        ).start()
    gall[chip] = gvec[...]
    core_copy.wait_recv()

    def turn(n, _):
        cols = pl.ds(pl.multiple_of(n * 128, 128), 128)
        v = qall[:, :, :, :, :, cols].astype(F32).reshape(1024, 128)
        qt[cols, :] = v.T.astype(BF16)
        return 0

    lax.fori_loop(0, C // 128, turn, 0)
    qt_store = load(qt, qt_out, 15)
    qt_store.start()
    await_bytes(gall.at[pl.ds(0, CHIPS - 1)], gsem.at[1])
    own_half = pltpu.make_async_copy(gall, g_out.at[core], hsem.at[13])
    own_half.start()
    grads_copy = pltpu.make_async_remote_copy(
        src_ref=gall, dst_ref=g_out.at[core], send_sem=gsem.at[2], recv_sem=gsem.at[3],
        device_id=cross_peer(0), device_id_type=MESH,
    )
    grads_copy.start()
    grads_copy.wait_recv()
    own_half.wait()
    qt_store.wait()
    keys_store.wait()

    await_bytes(tabv.at[pl.ds(0, 3)], tsem.at[0])
    for phase in range(4):
        q_wait(phase, 0)
    core_copy.wait_send()
    for r in range(ROUNDS):
        await_bytes(ra[r].at[pl.ds(0, PLANE - 1)], asem.at[0, r])
        await_bytes(rb.at[r, pl.ds(0, LINE - 1)], bsem.at[0, r])
    await_bytes(gall.at[pl.ds(0, CHIPS - 1)], gsem.at[0])
    grads_copy.wait_send()


def last(keys_ref, q_ref, g_ref, keys_out, grad_out, keys_v, q_v, g_v, out_v, sem):
    tall = C // PIECES

    def rows(n):
        return pl.ds(n * tall, tall)

    keys_in = pltpu.make_async_copy(keys_ref, keys_v, sem.at[0])
    g_in = pltpu.make_async_copy(g_ref, g_v, sem.at[1])
    q_in = [pltpu.make_async_copy(q_ref.at[rows(n)], q_v.at[n], sem.at[2 + n]) for n in range(PIECES)]
    g_in.start()
    for d in q_in:
        d.start()
    keys_in.start()
    stores = []
    g_in.wait()
    for n in range(PIECES):
        q_in[n].wait()
        out_v[n] = jnp.dot(q_v[n], g_v[...], preferred_element_type=F32)
        d = pltpu.make_async_copy(out_v.at[n], grad_out.at[rows(n)], sem.at[2 + PIECES + n])
        d.start()
        stores.append(d)
    keys_in.wait()
    d = pltpu.make_async_copy(keys_v, keys_out, sem.at[0])
    d.start()
    for e in stores:
        e.wait()
    d.wait()


def local(
    key_feats, clip_starts, shuffle, query_feats, conv_time, conv_space, conv_expand,
    gain_one, shift_one, gain_two, shift_two, gain_three, shift_three, w_key, w_query, queue,
):
    hbm = pl.BlockSpec(memory_space=pltpu.HBM)
    V = pltpu.VMEM
    DMA = pltpu.SemaphoreType.DMA
    rows = [v.reshape(1, -1) for v in (gain_one, shift_one, gain_two, shift_two, gain_three, shift_three)]
    keys, q_t, grads = pl.pallas_call(
        kernel,
        name="moco",
        out_shape=(
            jax.ShapeDtypeStruct((CLIPS, EMB), BF16),
            jax.ShapeDtypeStruct((C, 1024), BF16),
            jax.ShapeDtypeStruct((2, CHIPS, CLIPS, EMB), BF16),
        ),
        in_specs=[hbm] * 16,
        out_specs=(hbm, hbm, hbm),
        scratch_shapes=[
            [V((CLIPS, TF, SPOTS, KC), BF16) for _ in range(NK)],
            V((2, NK, 3, KC, 256), BF16),
            V((4, ROWS, 128), F32),
            V((4, ROWS, 128), F32),
            V((SIDE, SIDE + 2, 64, INNER), BF16),
            V((9, INNER, INNER), BF16),
            V((ROWS, INNER), BF16),
            V((4, INNER, INNER), BF16),
            V((4, ROWS, INNER), F32),
            V((QUEUE, EMB), BF16),
            V((2, 4, 4, 4, CLIPS, C), BF16),
            V((C, 1024), BF16),
            V((C, EMB), BF16),
            V((C, EMB), BF16),
            V((5, 8, 128), I32),
            pltpu.SMEM((5, 8, 128), I32),
            pltpu.SMEM((2, LINE), I32),
            V((ROUNDS, 8, 128), F32),
            [V((PLANE, 8, 128), F32) for _ in range(ROUNDS)],
            V((ROUNDS, LINE - 1, 8, 128), F32),
            V((ROUNDS, LINE - 1, 8, 128), F32),
            V((CLIPS, C), BF16),
            V((CHIPS, CLIPS, EMB), BF16),
            V((CLIPS, 8, C), F32),
            V((CLIPS, EMB), BF16),
            V((CLIPS, EMB), BF16),
            pltpu.SMEM((CLIPS,), I32),
            V((1, PEERS), I32),
            *[V((1, n), F32) for n in (INNER,) * 4 + (C,) * 2],
            DMA((34,)),
            DMA((2, ROUNDS)),
            DMA((2, ROUNDS)),
            DMA((4,)),
            DMA((2,)),
            DMA((2, 3, 4)),
            DMA((2,)),
        ],
        compiler_params=pltpu.CompilerParams(
            collective_id=0, has_side_effects=True, vmem_limit_bytes=67043328
        ),
    )(
        clip_starts, key_feats, shuffle, query_feats, conv_time, conv_space, conv_expand,
        *rows, w_key, w_query, queue,
    )
    return pl.pallas_call(
        last,
        name="last",
        out_shape=(jax.ShapeDtypeStruct((CLIPS, EMB), BF16), jax.ShapeDtypeStruct((C, EMB), F32)),
        in_specs=[hbm] * 3,
        out_specs=(hbm, hbm),
        scratch_shapes=[
            V((CLIPS, EMB), BF16),
            V((PIECES, C // PIECES, 1024), BF16),
            V((1024, EMB), BF16),
            V((PIECES, C // PIECES, EMB), F32),
            DMA((2 + 2 * PIECES,)),
        ],
    )(keys, q_t, grads.reshape(1024, EMB))


def solution(mesh):
    placed = (
        (P(("dp", "bn"), None, None, None), P(("dp", "bn")), P("bn", None), P(("dp", "bn"), None)) + (P(),) * 12
    )
    return jax.shard_map(
        local, mesh=mesh, in_specs=placed, out_specs=(P(("dp", "bn"), None), P()), check_vma=False
    )
```
